256 devices in a mesh: seq: 64 (over z, x, core), head: 4 (over y).
Axes of the slice: x: 4, y: 4, z: 8, core: 2. Of those that a mesh axis runs over, the one named last changes fastest.
Arguments:
- queries: bfloat16 [32768, 4096], P('seq', 'head'), may hold values from -6 to 6
- keys: bfloat16 [32768, 4096], P('seq', 'head'), may hold values from -6 to 6
- values: bfloat16 [32768, 4096], P('seq', 'head'), may hold values from -6 to 6
- level_weights: float32 [32, 9, 32768], P('head', None, 'seq'), may hold values from 0.5 to 1.5
- out_weight: bfloat16 [4096, 4096], P('head'), may hold values from -0.125 to 0.125
Outputs:
- mixed: bfloat16 [32768, 4096], P('seq', 'head')
The draws below stay inside these ranges and needn't reach their ends.
All inputs are finite; a program needn't handle non-finite values.
Results may differ from the reference program's by a relative error of at most 0.017.
Values may be sent and summed in bfloat16 or wider, within the bound.
A program may use at most 128 MiB of HBM per device.

```python
import jax
import jax.numpy as jnp
from jax import lax

D = 4096
H = 32
DH = 128
BLOCK = 128
LEVELS = 9
TOKENS = 32768
N_HEAD = 4


def spiked(drawn, stream_key, source, target, blocks, factor):
    def block_of(axis_at):
        return (jnp.arange(drawn.shape[axis_at]) // (drawn.shape[axis_at] // blocks)).reshape((-1,) + (1,) * (drawn.ndim - 1 - axis_at))

    one_side = jax.random.permutation(stream_key, blocks)[block_of(target)]
    far = (block_of(target) + blocks // 2) % blocks
    return jnp.where((block_of(source) == one_side) | (block_of(source) == far), factor * drawn, drawn)


def level_of(key, extent, split, smallest, high):
    def one(dim, shards_of):
        steps = jax.random.uniform(jax.random.fold_in(jax.random.fold_in(key, 6), dim), (shards_of,), jnp.float32, smallest / len(split), high / len(split))
        return jnp.repeat(jnp.exp(steps), extent[dim] // shards_of).reshape((-1,) + (1,) * (len(extent) - dim - 1))

    level = one(*split[0])
    for cut in split[1:]:
        level = level * one(*cut)
    return level


def bell_draw(key, shape, deviation, limit, pieces=(), kind=jnp.bfloat16):
    gain = level_of(key, shape, pieces, -0.22, 0.18) if pieces else 1.0
    entries = jax.random.normal(key, shape, jnp.float32) * deviation * gain
    return jnp.minimum(jnp.maximum(entries, -limit), limit).astype(kind)


def bell_draw_with(stream_key, dims, deviation, reach, cuts, heavy, kind=jnp.bfloat16):
    result = deviation * jax.random.normal(stream_key, dims, jnp.float32)
    if cuts:
        result = result * level_of(stream_key, dims, cuts, -0.22, 0.18)
    return jnp.clip(spiked(result, jax.random.fold_in(stream_key, 3), *heavy), -reach, reach).astype(kind)


def setup_inputs(seed: int = 0) -> dict:
    key_list = jax.random.split(jax.random.key(seed), 6)
    return {
        "queries": bell_draw(key_list[0], (TOKENS, H * DH), 1.0, 6.0, ((0, 64), (1, 4))),
        "keys": bell_draw(key_list[1], (TOKENS, H * DH), 1.0, 6.0, ((0, 64), (1, 4))),
        "values": bell_draw(key_list[2], (TOKENS, H * DH), 1.0, 6.0, ((0, 64), (1, 4))),
        "level_weights": jnp.clip(0.5 + 1.0 * jax.random.uniform(key_list[3], (H, LEVELS, TOKENS), jnp.float32) ** level_of(key_list[3], (H, LEVELS, TOKENS), ((0, 4), (2, 64)), -0.2, 0.2), 0.5, 1.5),
        "out_weight": bell_draw_with(key_list[4], (H * DH, D), (H * DH) ** -0.5, 0.125, ((0, 4),), (0, 1, 4, 2.0)),
    }


epsilon = 1e-06

def unit_rows(matrix):
    shaped = matrix.astype(jnp.float32).reshape(matrix.shape[0], H, DH)
    return (shaped / jnp.sqrt(lax.optimization_barrier(jnp.sum(shaped * shaped, axis=-1, keepdims=True)) + epsilon)).astype(jnp.bfloat16)

def head_mix(inputs):
    q_head, k_head, v_head, lam_head = inputs
    block_count = TOKENS // BLOCK
    q_blocks = q_head.astype(jnp.float32).reshape(block_count, BLOCK, DH)
    k_blocks = k_head.astype(jnp.float32).reshape(block_count, BLOCK, DH)
    v_blocks = v_head.astype(jnp.float32).reshape(block_count, BLOCK, DH)
    scores = jnp.einsum('bid,bjd->bij', q_blocks, k_blocks)
    row_pos = jnp.arange(BLOCK, dtype=jnp.int32)
    causal = row_pos[:, None] >= row_pos[None, :]
    level_zero = lam_head[0].reshape(block_count, BLOCK, 1)
    weights = jnp.where(causal[None], scores * level_zero, 0.0).astype(jnp.bfloat16)
    totals = jnp.einsum('bij,bjd->bid', weights.astype(jnp.float32), v_blocks)
    states = jnp.einsum('bjd,bje->bde', k_blocks, v_blocks)
    for level_idx in range(1, LEVELS):
        span_size = 2 ** (level_idx - 1)
        if 2 * span_size > block_count:
            break
        group_count = block_count // (2 * span_size)
        left_sum = states.reshape(group_count, 2, span_size, DH, DH)[:, 0].sum(axis=1).astype(jnp.bfloat16)
        right_rows = q_blocks.reshape(group_count, 2, span_size * BLOCK, DH)[:, 1]
        read_out = jnp.einsum('gid,gde->gie', right_rows, left_sum.astype(jnp.float32))
        factor = lam_head[level_idx].reshape(group_count, 2, span_size * BLOCK)[:, 1]
        read_out = read_out * factor[..., None]
        totals = totals + jnp.stack([jnp.zeros_like(read_out), read_out], axis=1).reshape(block_count, BLOCK, DH)
    return totals.reshape(TOKENS, DH)

def reference(queries, keys, values, level_weights, out_weight):
    q_unit = unit_rows(queries).transpose(1, 0, 2)
    k_unit = unit_rows(keys).transpose(1, 0, 2)
    v_rows = values.reshape(TOKENS, H, DH).transpose(1, 0, 2)
    attended = lax.map(head_mix, (q_unit, k_unit, v_rows, level_weights)).transpose(1, 0, 2)
    normed = attended / jnp.sqrt(lax.optimization_barrier(jnp.mean(attended * attended, axis=-1, keepdims=True)) + epsilon)
    normed = normed.astype(jnp.bfloat16).reshape(TOKENS, H * DH)
    group_cols = H * DH // N_HEAD
    summed = jnp.zeros((TOKENS, D), jnp.float32)
    for group_idx in range(N_HEAD):
        lower = group_idx * group_cols
        product = jnp.dot(normed[:, lower:lower + group_cols], out_weight[lower:lower + group_cols], preferred_element_type=jnp.float32)
        summed = summed + product.astype(jnp.bfloat16).astype(jnp.float32)
    return summed.astype(jnp.bfloat16)
```

```python
import jax
import jax.numpy as jnp
from jax import lax
from jax.experimental import pallas as pl
from jax.experimental.pallas import tpu as pltpu
from jax.sharding import PartitionSpec as P

BLOCK = 128
EPS = 1e-06
LINE = 8
CHIPS = 4
PLANES = 8
FAR = 6
BF = jnp.bfloat16
F32 = jnp.float32
MESH = pl.DeviceIdType.MESH


def dot(a, b):
    return jnp.dot(a, b, preferred_element_type=F32)


def kernel(
    q_hbm,
    k_hbm,
    v_hbm,
    lw_hbm,
    w_hbm,
    out_ref,
    q_v,
    k_v,
    v_v,
    lw_v,
    w_v,
    bst,
    stbuf,
    recv1,
    lowbuf,
    zrecv,
    states,
    qs,
    tot,
    nrm,
    p1s,
    p1r,
    p2s,
    p2r,
    mine,
    own,
    in_sem,
    p1_s,
    p1_r,
    core_s,
    core_r,
    z_s,
    z_r,
    low_s,
    low_r,
    hi_s,
    hi_r,
    y1_s,
    y1_r,
    y2_s,
    y2_r,
):
    heads = stbuf.shape[0]
    tok = q_v.shape[0]
    nblk = tok // BLOCK
    p = lax.axis_index("seq")
    y = lax.axis_index("head")
    z = p // LINE
    d = p % LINE
    core = d % 2
    x = d // 2
    pa = y + 1 - 2 * (y % 2)
    pb = 3 - y
    opp = (y + 2) % 4

    def line(e):
        return (z * LINE + e, y)

    def local_in(i, src, dst):
        return pltpu.make_async_copy(src, dst, in_sem.at[i])

    cps = [
        local_in(0, k_hbm, k_v),
        local_in(1, v_hbm, v_v),
        local_in(2, q_hbm, q_v),
        local_in(3, lw_hbm, lw_v),
        local_in(4, w_hbm, w_v),
    ]
    for c in cps:
        c.start()

    barrier = pltpu.get_barrier_semaphore()
    for i in range(1, LINE):
        pl.semaphore_signal(barrier, inc=1, device_id=line((d + i) % LINE), device_id_type=MESH)
    for i in range(1, PLANES):
        pl.semaphore_signal(
            barrier, inc=1, device_id=(((z + i) % PLANES) * LINE + d, y), device_id_type=MESH
        )
    for t in (pa, pb):
        pl.semaphore_signal(barrier, inc=1, device_id=(p, t), device_id_type=MESH)

    def cols(h):
        return pl.ds(pl.multiple_of(h * 128, 128), 128)

    @pl.when(core == 0)
    def _():
        states[:, pl.ds(0, 128), :] = jnp.zeros((heads, 128, 128), BF)

    cps[0].wait()
    cps[1].wait()

    def key_head(h, _):
        kf = k_v[:, cols(h)].astype(F32)
        ku = (kf * lax.rsqrt(jnp.sum(kf * kf, axis=-1, keepdims=True) + EPS)).astype(BF)
        k_v[:, cols(h)] = ku
        vv = v_v[:, cols(h)]
        s = [
            lax.dot_general(
                ku[b * BLOCK : (b + 1) * BLOCK],
                vv[b * BLOCK : (b + 1) * BLOCK],
                (((0,), (0,)), ((), ())),
                preferred_element_type=F32,
            )
            for b in range(nblk)
        ]
        s01 = s[0] + s[1]
        bst[h, 0] = s[0].astype(BF)
        bst[h, 1] = s[2].astype(BF)
        bst[h, 2] = s01.astype(BF)
        stbuf[h] = (s01 + s[2] + s[3]).astype(BF)
        return 0

    lax.fori_loop(0, heads, key_head, 0)
    pl.semaphore_wait(barrier, LINE - 1 + PLANES - 1 + 2)

    def send1(e):
        return pltpu.make_async_remote_copy(
            src_ref=stbuf.at[e],
            dst_ref=recv1.at[d],
            send_sem=p1_s.at[e],
            recv_sem=p1_r.at[d],
            device_id=line(e),
            device_id_type=MESH,
        )

    for i in range(1, LINE):
        send1((d + i) % LINE).start()
    core_copy = pltpu.make_async_remote_copy(
        src_ref=stbuf,
        dst_ref=states.at[:, pl.ds(0, 128), :],
        send_sem=core_s,
        recv_sem=core_r,
        device_id=line(d + 1 - 2 * core),
        device_id_type=MESH,
    )

    @pl.when(core == 0)
    def _():
        core_copy.start()

    recv1[d] = stbuf[d]

    cps[2].wait()
    cps[3].wait()
    causal = lax.broadcasted_iota(jnp.int32, (BLOCK, BLOCK), 0) >= lax.broadcasted_iota(
        jnp.int32, (BLOCK, BLOCK), 1
    )

    def query_head(h, _):
        qf = q_v[:, cols(h)].astype(F32)
        qu = (qf * lax.rsqrt(jnp.sum(qf * qf, axis=-1, keepdims=True) + EPS)).astype(BF)
        q_v[:, cols(h)] = qu
        lwt = lw_v[h].T
        for b in range(nblk):
            rows = pl.ds(b * BLOCK, BLOCK)
            part = slice(b * BLOCK, (b + 1) * BLOCK)
            qb = qu[part]
            s = lax.dot_general(
                qb, k_v[rows, cols(h)], (((1,), (1,)), ((), ())), preferred_element_type=F32
            )
            wgt = jnp.where(causal, s * lwt[part, 0:1], 0.0).astype(BF)
            acc = dot(wgt, v_v[rows, cols(h)])
            if b % 2 == 1:
                acc = acc + dot(qb, bst[h, b // 2]) * lwt[part, 1:2]
            if b >= 2:
                acc = acc + dot(qb, bst[h, 2]) * lwt[part, 2:3]
            tot[rows, cols(h)] = acc
        return 0

    lax.fori_loop(0, heads, query_head, 0)

    for i in range(1, LINE):
        e = (d + i) % LINE
        pltpu.make_async_remote_copy(
            src_ref=stbuf.at[e],
            dst_ref=recv1.at[e],
            send_sem=p1_s.at[e],
            recv_sem=p1_r.at[e],
            device_id=line(e),
            device_id_type=MESH,
        ).wait_recv()
    pair = [recv1[2 * c].astype(F32) + recv1[2 * c + 1].astype(F32) for c in range(CHIPS)]
    half = pair[0] + pair[1]
    zrecv[z] = (half + pair[2] + pair[3]).astype(BF)

    def zsend(t):
        return pltpu.make_async_remote_copy(
            src_ref=zrecv.at[z],
            dst_ref=zrecv.at[z],
            send_sem=z_s.at[t],
            recv_sem=z_r.at[z],
            device_id=(t * LINE + d, y),
            device_id_type=MESH,
        )

    for t in range(1, PLANES):

        @pl.when(z < t)
        def _():
            zsend(t).start()

    none = jnp.zeros((128, 128), BF)
    for c in range(CHIPS):
        lowbuf[c, 0] = pair[c - 1].astype(BF) if c % 2 else none
        lowbuf[c, 1] = half.astype(BF) if c >= 2 else none

    low_rows = pl.ds(128, 256)
    hi_rows = pl.ds(384, 384)

    def spread(src, rows, peer, s_sem, i, r_sem, h):
        return pltpu.make_async_remote_copy(
            src_ref=src,
            dst_ref=states.at[h, rows, :],
            send_sem=s_sem.at[i],
            recv_sem=r_sem.at[h],
            device_id=line(peer),
            device_id_type=MESH,
        )

    mate = d + 1 - 2 * core
    sends = []
    states[d, pl.ds(128, 128), :] = lowbuf[x, 0]
    states[d, pl.ds(256, 128), :] = lowbuf[x, 1]
    lowsrc = lowbuf.reshape(CHIPS, 256, 128)
    for i in range(1, CHIPS):
        c = (x + i) % CHIPS
        cp = spread(lowsrc.at[c], low_rows, c * 2 + core, low_s, i, low_r, d)
        cp.start()
        sends.append(cp)
    cp = spread(lowsrc.at[x], low_rows, mate, low_s, 0, low_r, d)
    cp.start()
    sends.append(cp)

    def scale_head(h, _):
        quf = q_v[:, cols(h)].astype(F32)
        lwt = lw_v[h].T
        for lv in range(FAR):
            qs[h, :, lv * 128 : (lv + 1) * 128] = (quf * lwt[:, 3 + lv : 4 + lv]).astype(BF)
        return 0

    lax.fori_loop(0, heads, scale_head, 0)

    def forward(rows, s_sem, r_sem):
        for i in range(1, CHIPS):
            c = (x + CHIPS - i) % CHIPS
            h = c * 2 + core
            spread(states.at[h, rows, :], rows, mate, s_sem, 0, r_sem, h).wait_recv()
            cp = spread(states.at[h, rows, :], rows, mate, s_sem, CHIPS + i - 1, r_sem, h)
            cp.start()
            sends.append(cp)

    def landed(rows, s_sem, r_sem):
        for i in range(CHIPS):
            h = i * 2 + 1 - core
            spread(states.at[h, rows, :], rows, mate, s_sem, 0, r_sem, h).wait_recv()

    forward(low_rows, low_s, low_r)

    for s in range(PLANES - 1):

        @pl.when(s < z)
        def _():
            pltpu.make_async_remote_copy(
                src_ref=zrecv.at[s],
                dst_ref=zrecv.at[s],
                send_sem=z_s.at[0],
                recv_sem=z_r.at[s],
                device_id=(s * LINE + d, y),
                device_id_type=MESH,
            ).wait_recv()

    def put(row, val):
        states[d, pl.ds(row, 128), :] = val

    base = (z // 4) * 4

    @pl.when(z % 2 == 1)
    def _():
        put(384, zrecv[z - 1])

    @pl.when(z % 2 == 0)
    def _():
        put(384, none)

    @pl.when((z // 2) % 2 == 1)
    def _():
        put(512, (zrecv[base].astype(F32) + zrecv[base + 1].astype(F32)).astype(BF))

    @pl.when((z // 2) % 2 == 0)
    def _():
        put(512, none)

    @pl.when(z >= 4)
    def _():
        q4 = [zrecv[i].astype(F32) for i in range(4)]
        put(640, (q4[0] + q4[1] + q4[2] + q4[3]).astype(BF))

    @pl.when(z < 4)
    def _():
        put(640, none)

    mysrc = states.at[d, hi_rows, :]
    for i in range(1, CHIPS):
        c = (x + i) % CHIPS
        cp = spread(mysrc, hi_rows, c * 2 + core, hi_s, i, hi_r, d)
        cp.start()
        sends.append(cp)
    cp = spread(mysrc, hi_rows, mate, hi_s, 0, hi_r, d)
    cp.start()
    sends.append(cp)

    landed(low_rows, low_s, low_r)

    @pl.when(core == 1)
    def _():
        core_copy.wait_recv()

    def low_head(h, _):
        tot[:, cols(h)] += dot(qs[h, :, 0:384], states[h, 0:384, :])
        return 0

    lax.fori_loop(0, heads, low_head, 0)

    forward(hi_rows, hi_s, hi_r)
    landed(hi_rows, hi_s, hi_r)

    def norm_head(h, _):
        a = tot[:, cols(h)] + dot(qs[h, :, 384:768], states[h, 384:768, :])
        m = jnp.mean(a * a, axis=-1, keepdims=True)
        nrm[:, cols(h)] = (a * lax.rsqrt(m + EPS)).astype(BF)
        return 0

    lax.fori_loop(0, heads, norm_head, 0)
    cps[4].wait()

    top = tok // 2
    wide = out_ref.shape[1]
    tiles = mine.shape[1]
    tw = wide // tiles

    def tile_product(block, t):
        lo = pl.multiple_of(block * wide + t * tw, tw)
        return dot(nrm[...], w_v[:, pl.ds(lo, tw)])

    def y1(side, i):
        return pltpu.make_async_remote_copy(
            src_ref=p1s.at[side, i],
            dst_ref=p1r.at[side, i],
            send_sem=y1_s.at[side, i],
            recv_sem=y1_r.at[side, i],
            device_id=(p, (pa, pb)[side]),
            device_id_type=MESH,
        )

    def y2(side, i):
        return pltpu.make_async_remote_copy(
            src_ref=p2s.at[side, i],
            dst_ref=p2r.at[side, i],
            send_sem=y2_s.at[side, i],
            recv_sem=y2_r.at[side, i],
            device_id=(p, (pa, pb)[side]),
            device_id_type=MESH,
        )

    def far_tile(t, _):
        prod = tile_product(opp, t)
        p1s[0, t] = prod[:top].astype(BF)
        y1(0, t).start()
        p1s[1, t] = prod[top:].astype(BF)
        y1(1, t).start()
        return 0

    lax.fori_loop(0, tiles, far_tile, 0)

    def side_tile(t, _):
        prod = tile_product(pa, t)
        p1s[0, tiles + t] = prod[:top].astype(BF)
        y1(0, tiles + t).start()
        mine[0, t] = prod[top:]
        prod = tile_product(pb, t)
        p1s[1, tiles + t] = prod[top:].astype(BF)
        y1(1, tiles + t).start()
        mine[1, t] = prod[:top]
        return 0

    lax.fori_loop(0, tiles, side_tile, 0)

    def second(t, _):
        y1(1, t).wait_recv()
        p2s[0, t] = (mine[0, t] + p1r[1, t].astype(F32)).astype(BF)
        y2(0, t).start()
        y1(0, t).wait_recv()
        p2s[1, t] = (mine[1, t] + p1r[0, t].astype(F32)).astype(BF)
        y2(1, t).start()
        return 0

    def own_tile(t, _):
        own[t] = tile_product(y, t)
        return 0

    lax.fori_loop(0, tiles, own_tile, 0)
    lax.fori_loop(0, tiles, second, 0)

    def last(t, _):
        lanes = pl.ds(pl.multiple_of(t * tw, tw), tw)
        y1(0, tiles + t).wait_recv()
        y2(1, t).wait_recv()
        out_ref[pl.ds(0, top), lanes] = (
            own[t, pl.ds(0, top), :] + p1r[0, tiles + t].astype(F32) + p2r[1, t].astype(F32)
        ).astype(BF)
        y1(1, tiles + t).wait_recv()
        y2(0, t).wait_recv()
        out_ref[pl.ds(top, top), lanes] = (
            own[t, pl.ds(top, top), :] + p1r[1, tiles + t].astype(F32) + p2r[0, t].astype(F32)
        ).astype(BF)
        return 0

    lax.fori_loop(0, tiles, last, 0)

    for i in range(1, LINE):
        send1((d + i) % LINE).wait_send()

    @pl.when(core == 0)
    def _():
        core_copy.wait_send()

    for t in range(1, PLANES):

        @pl.when(z < t)
        def _():
            zsend(t).wait_send()

    for cp in sends:
        cp.wait_send()
    for side in range(2):

        def drain(i, _):
            y1(side, i).wait_send()
            return 0

        lax.fori_loop(0, 2 * tiles, drain, 0)

        def drain2(i, _):
            y2(side, i).wait_send()
            return 0

        lax.fori_loop(0, tiles, drain2, 0)


def local(queries, keys, values, level_weights, out_weight):
    tok, width = queries.shape
    heads, levels, _ = level_weights.shape
    tiles = 4
    top = tok // 2
    tw = width // tiles
    dma = pltpu.SemaphoreType.DMA
    scratch = [
        pltpu.VMEM((tok, width), BF),
        pltpu.VMEM((tok, width), BF),
        pltpu.VMEM((tok, width), BF),
        pltpu.VMEM((heads, levels, tok), F32),
        pltpu.VMEM(out_weight.shape, BF),
        pltpu.VMEM((heads, 3, 128, 128), BF),
        pltpu.VMEM((heads, 128, 128), BF),
        pltpu.VMEM((LINE, 128, 128), BF),
        pltpu.VMEM((CHIPS, 2, 128, 128), BF),
        pltpu.VMEM((PLANES, 128, 128), BF),
        pltpu.VMEM((heads, FAR * 128, 128), BF),
        pltpu.VMEM((heads, tok, FAR * 128), BF),
        pltpu.VMEM((tok, width), F32),
        pltpu.VMEM((tok, width), BF),
        pltpu.VMEM((2, 2 * tiles, top, tw), BF),
        pltpu.VMEM((2, 2 * tiles, top, tw), BF),
        pltpu.VMEM((2, tiles, top, tw), BF),
        pltpu.VMEM((2, tiles, top, tw), BF),
        pltpu.VMEM((2, tiles, top, tw), F32),
        pltpu.VMEM((tiles, tok, tw), F32),
        dma((5,)),
        dma((LINE,)),
        dma((LINE,)),
        dma,
        dma,
        dma((PLANES,)),
        dma((PLANES,)),
        dma((2 * CHIPS,)),
        dma((LINE,)),
        dma((2 * CHIPS,)),
        dma((LINE,)),
        dma((2, 2 * tiles)),
        dma((2, 2 * tiles)),
        dma((2, tiles)),
        dma((2, tiles)),
    ]
    return pl.pallas_call(
        kernel,
        out_shape=jax.ShapeDtypeStruct((tok, width), BF),
        in_specs=[pl.BlockSpec(memory_space=pl.ANY)] * 5,
        out_specs=pl.BlockSpec(memory_space=pltpu.VMEM),
        scratch_shapes=scratch,
        compiler_params=pltpu.CompilerParams(
            collective_id=0, has_side_effects=True, vmem_limit_bytes=60 * 1024 * 1024
        ),
    )(queries, keys, values, level_weights, out_weight)


def solution(mesh):
    in_specs = (
        P("seq", "head"),
        P("seq", "head"),
        P("seq", "head"),
        P("head", None, "seq"),
        P("head", None),
    )
    out_specs = P("seq", "head")
    return jax.shard_map(local, mesh=mesh, in_specs=in_specs, out_specs=out_specs, check_vma=False)
```

```python
import jax
import jax.numpy as jnp
from jax import lax
from jax.experimental import pallas as pl
from jax.experimental.pallas import tpu as pltpu
from jax.sharding import PartitionSpec as P

BLOCK = 128
EPS = 1e-06
LINE = 8
CHIPS = 4
PLANES = 8
FAR = 6
NEAR = (1, 2, 3, PLANES - 3, PLANES - 2, PLANES - 1)
TAKERS = {0: (3, 2, 1), 1: (3, 2, 0), 2: (3, 0), 3: (0,), 4: (7, 6, 5), 5: (7, 6), 6: (7,)}
ROOTS = {3: (5, 4), 0: (6, 7)}
BF = jnp.bfloat16
F32 = jnp.float32
MESH = pl.DeviceIdType.MESH


def dot(a, b):
    return jnp.dot(a, b, preferred_element_type=F32)


def kernel(
    q_hbm,
    k_hbm,
    v_hbm,
    lw_hbm,
    w_hbm,
    out_ref,
    q_v,
    k_v,
    v_v,
    lw_v,
    lw_t,
    w_v,
    bst,
    stbuf,
    recv1,
    lowbuf,
    zrecv,
    states,
    qs,
    tot,
    nrm,
    p1s,
    p1r,
    p2s,
    p2r,
    mine,
    own,
    in_sem,
    p1_s,
    p1_r,
    core_s,
    core_r,
    z_s,
    z_r,
    low_s,
    low_r,
    mid_s,
    mid_r,
    hi_s,
    hi_r,
    y1_s,
    y1_r,
    y2_s,
    y2_r,
):
    heads = stbuf.shape[0]
    tok = q_v.shape[0]
    nblk = tok // BLOCK
    p = lax.axis_index("seq")
    y = lax.axis_index("head")
    z = p // LINE
    d = p % LINE
    core = d % 2
    x = d // 2
    pa = y + 1 - 2 * (y % 2)
    pb = 3 - y
    opp = (y + 2) % 4

    def line(e):
        return (z * LINE + e, y)

    def local_in(i, src, dst):
        return pltpu.make_async_copy(src, dst, in_sem.at[i])

    cps = [
        local_in(0, k_hbm, k_v),
        local_in(1, v_hbm, v_v),
        local_in(2, q_hbm, q_v),
        local_in(3, lw_hbm, lw_v),
        local_in(4, w_hbm, w_v),
    ]
    for c in cps:
        c.start()

    barrier = pltpu.get_barrier_semaphore()
    for i in range(1, LINE):
        pl.semaphore_signal(barrier, inc=1, device_id=line((d + i) % LINE), device_id_type=MESH)
    for i in NEAR:
        pl.semaphore_signal(
            barrier, inc=1, device_id=(((z + i) % PLANES) * LINE + d, y), device_id_type=MESH
        )
    for t in (pa, pb):
        pl.semaphore_signal(barrier, inc=1, device_id=(p, t), device_id_type=MESH)

    def cols(h):
        return pl.ds(pl.multiple_of(h * 128, 128), 128)

    @pl.when(core == 0)
    def _():
        states[:, pl.ds(0, 128), :] = jnp.zeros((heads, 128, 128), BF)

    @pl.when(x % 2 == 0)
    def _():
        states[:, pl.ds(128, 128), :] = jnp.zeros((heads, 128, 128), BF)

    @pl.when(x < 2)
    def _():
        states[:, pl.ds(256, 128), :] = jnp.zeros((heads, 128, 128), BF)

    cps[0].wait()
    cps[1].wait()

    def key_head(h, _):
        kf = k_v[:, cols(h)].astype(F32)
        ku = (kf * lax.rsqrt(jnp.sum(kf * kf, axis=-1, keepdims=True) + EPS)).astype(BF)
        k_v[:, cols(h)] = ku
        vv = v_v[:, cols(h)]
        s = [
            lax.dot_general(
                ku[b * BLOCK : (b + 1) * BLOCK],
                vv[b * BLOCK : (b + 1) * BLOCK],
                (((0,), (0,)), ((), ())),
                preferred_element_type=F32,
            )
            for b in range(nblk)
        ]
        s01 = s[0] + s[1]
        bst[h, 0] = s[0].astype(BF)
        bst[h, 1] = s[2].astype(BF)
        bst[h, 2] = s01.astype(BF)
        stbuf[h] = (s01 + s[2] + s[3]).astype(BF)
        return 0

    lax.fori_loop(0, heads, key_head, 0, unroll=True)
    pl.semaphore_wait(barrier, LINE - 1 + len(NEAR) + 2)

    def send1(e):
        return pltpu.make_async_remote_copy(
            src_ref=stbuf.at[e],
            dst_ref=recv1.at[d],
            send_sem=p1_s.at[e],
            recv_sem=p1_r.at[d],
            device_id=line(e),
            device_id_type=MESH,
        )

    for i in range(1, LINE):
        send1((d + i) % LINE).start()
    core_copy = pltpu.make_async_remote_copy(
        src_ref=stbuf,
        dst_ref=states.at[:, pl.ds(0, 128), :],
        send_sem=core_s,
        recv_sem=core_r,
        device_id=line(d + 1 - 2 * core),
        device_id_type=MESH,
    )

    @pl.when(core == 0)
    def _():
        core_copy.start()

    recv1[d] = stbuf[d]

    cps[2].wait()
    cps[3].wait()
    lw_all = lw_v[...].reshape(lw_v.shape[0] * heads, tok)
    lw_t[...] = jnp.concatenate([lw_all, jnp.zeros((128 - lw_all.shape[0], tok), F32)], axis=0).T

    def level_columns(h):
        return pltpu.roll(lw_t[...], lax.rem(128 - h, 128), 1)

    causal = lax.broadcasted_iota(jnp.int32, (BLOCK, BLOCK), 0) >= lax.broadcasted_iota(
        jnp.int32, (BLOCK, BLOCK), 1
    )

    def query_head(h, _):
        qf = q_v[:, cols(h)].astype(F32)
        qu = (qf * lax.rsqrt(jnp.sum(qf * qf, axis=-1, keepdims=True) + EPS)).astype(BF)
        q_v[:, cols(h)] = qu
        lwt = level_columns(h)
        for b in range(nblk):
            rows = pl.ds(b * BLOCK, BLOCK)
            part = slice(b * BLOCK, (b + 1) * BLOCK)
            qb = qu[part]
            s = lax.dot_general(
                qb, k_v[rows, cols(h)], (((1,), (1,)), ((), ())), preferred_element_type=F32
            )
            wgt = jnp.where(causal, s * lwt[part, 0:1], 0.0).astype(BF)
            acc = dot(wgt, v_v[rows, cols(h)])
            if b % 2 == 1:
                acc = acc + dot(qb, bst[h, b // 2]) * lwt[part, 8:9]
            if b >= 2:
                acc = acc + dot(qb, bst[h, 2]) * lwt[part, 16:17]
            tot[rows, cols(h)] = acc
        return 0

    lax.fori_loop(0, heads, query_head, 0, unroll=True)

    for i in range(1, LINE):
        e = (d + i) % LINE
        pltpu.make_async_remote_copy(
            src_ref=stbuf.at[e],
            dst_ref=recv1.at[e],
            send_sem=p1_s.at[e],
            recv_sem=p1_r.at[e],
            device_id=line(e),
            device_id_type=MESH,
        ).wait_recv()
    pair = [recv1[2 * c].astype(F32) + recv1[2 * c + 1].astype(F32) for c in range(CHIPS)]
    half = pair[0] + pair[1]
    zrecv[z] = (half + pair[2] + pair[3]).astype(BF)

    def zcopy(slot, src, t):
        return pltpu.make_async_remote_copy(
            src_ref=zrecv.at[src],
            dst_ref=zrecv.at[src],
            send_sem=z_s.at[slot],
            recv_sem=z_r.at[src],
            device_id=(t * LINE + d, y),
            device_id_type=MESH,
        )

    for src, takers in TAKERS.items():

        @pl.when(z == src)
        def _():
            for slot, t in enumerate(takers):
                zcopy(slot, src, t).start()

    none = jnp.zeros((128, 128), BF)
    for c in range(CHIPS):
        lowbuf[c, pl.ds(0, 128), :] = pair[c - 1].astype(BF) if c % 2 else none
        lowbuf[c, pl.ds(128, 128), :] = half.astype(BF) if c >= 2 else none

    mid_rows = pl.ds(384, 256)
    hi_rows = pl.ds(640, 128)

    def spread(src, rows, peer, s_sem, i, r_sem, h):
        return pltpu.make_async_remote_copy(
            src_ref=src,
            dst_ref=states.at[h, rows, :],
            send_sem=s_sem.at[i],
            recv_sem=r_sem.at[h],
            device_id=line(peer),
            device_id_type=MESH,
        )

    mate = d + 1 - 2 * core
    sends = []
    states[d, pl.ds(128, 256), :] = lowbuf[x]
    def low_copy(c, slot):
        first = 0 if c % 2 else 1
        count = 2 if c == 3 else 1
        return pltpu.make_async_remote_copy(
            src_ref=lowbuf.at[c, pl.ds(first * 128, count * 128), :],
            dst_ref=states.at[d, pl.ds(128 + first * 128, count * 128), :],
            send_sem=low_s.at[slot],
            recv_sem=low_r.at[d],
            device_id=line(mate if slot == 0 else c * 2 + core),
            device_id_type=MESH,
        )

    for c in range(1, CHIPS):

        @pl.when(x != c)
        def _():
            low_copy(c, c).start()

        @pl.when(x == c)
        def _():
            low_copy(c, 0).start()

    def scaled(h, levels):
        quf = q_v[:, cols(h)].astype(F32)
        lwt = level_columns(h)
        for lv in levels:
            col = 8 * (3 + lv)
            qs[h, :, lv * 128 : (lv + 1) * 128] = (quf * lwt[:, col : col + 1]).astype(BF)
        return 0

    def scale_low(h, _):
        return scaled(h, range(0, 3))

    def scale_high(h, _):
        return scaled(h, range(3, FAR))

    lax.fori_loop(0, heads, scale_low, 0, unroll=True)

    def low_forward(c):
        first = 0 if c % 2 else 1
        count = 2 if c == 3 else 1
        rows = pl.ds(128 + first * 128, count * 128)
        for i in range(1, CHIPS):
            h = ((c + i) % CHIPS) * 2 + core
            spread(states.at[h, rows, :], rows, mate, low_s, 0, low_r, h).wait_recv()
            spread(states.at[h, rows, :], rows, mate, low_s, CHIPS + i - 1, low_r, h).start()

    def low_landed(c):
        first = 0 if c % 2 else 1
        count = 2 if c == 3 else 1
        rows = pl.ds(128 + first * 128, count * 128)
        for i in range(CHIPS):
            h = i * 2 + 1 - core
            spread(states.at[h, rows, :], rows, mate, low_s, 0, low_r, h).wait_recv()

    def along_line(rows, s_sem, r_sem):
        src = states.at[d, rows, :]
        for i in (2, 1, 3, 0):
            e = ((x + i) % CHIPS) * 2 + core if i else mate
            cp = spread(src, rows, e, s_sem, i, r_sem, d)
            cp.start()
            sends.append(cp)

    def forward(rows, s_sem, r_sem):
        for i in (1, 3, 2):
            h = ((x + i) % CHIPS) * 2 + core
            src = states.at[h, rows, :]
            spread(src, rows, mate, s_sem, 0, r_sem, h).wait_recv()
            cp = spread(src, rows, mate, s_sem, 3 + i, r_sem, h)
            cp.start()
            sends.append(cp)

    def landed(rows, s_sem, r_sem):
        for i in range(CHIPS):
            h = i * 2 + 1 - core
            spread(states.at[h, rows, :], rows, mate, s_sem, 0, r_sem, h).wait_recv()

    for t in range(PLANES):

        @pl.when(z == t)
        def _():
            for src, takers in TAKERS.items():
                if t in takers:
                    zcopy(0, src, t).wait_recv()

    def put(row, val):
        states[d, pl.ds(row, 128), :] = val

    for root, takers in ROOTS.items():

        @pl.when(z == root)
        def _():
            q4 = [zrecv[i].astype(F32) for i in range(4)]
            zrecv[PLANES] = (q4[0] + q4[1] + q4[2] + q4[3]).astype(BF)
            for slot, t in enumerate(takers):
                zcopy(3 + slot, PLANES, t).start()

    base = (z // 4) * 4

    @pl.when(z % 2 == 1)
    def _():
        put(384, zrecv[z - 1])

    @pl.when(z % 2 == 0)
    def _():
        put(384, none)

    @pl.when((z // 2) % 2 == 1)
    def _():
        put(512, (zrecv[base].astype(F32) + zrecv[base + 1].astype(F32)).astype(BF))

    @pl.when((z // 2) % 2 == 0)
    def _():
        put(512, none)

    along_line(mid_rows, mid_s, mid_r)
    lax.fori_loop(0, heads, scale_high, 0, unroll=True)
    for c in range(1, CHIPS):

        @pl.when(x == c)
        def _():
            low_forward(c)

    @pl.when(z >= 4)
    def _():
        zcopy(0, PLANES, 0).wait_recv()
        put(640, zrecv[PLANES])

    @pl.when(z < 4)
    def _():
        put(640, none)

    along_line(hi_rows, hi_s, hi_r)
    for c in range(1, CHIPS):

        @pl.when(x == c)
        def _():
            low_landed(c)

    @pl.when(core == 1)
    def _():
        core_copy.wait_recv()

    def low_head(h, _):
        tot[:, cols(h)] += dot(qs[h, :, 0:384], states[h, 0:384, :])
        return 0

    lax.fori_loop(0, heads, low_head, 0, unroll=True)

    forward(mid_rows, mid_s, mid_r)
    landed(mid_rows, mid_s, mid_r)

    def mid_head(h, _):
        tot[:, cols(h)] += dot(qs[h, :, 384:640], states[h, 384:640, :])
        return 0

    lax.fori_loop(0, heads, mid_head, 0, unroll=True)

    forward(hi_rows, hi_s, hi_r)
    landed(hi_rows, hi_s, hi_r)

    def norm_head(h, _):
        a = tot[:, cols(h)] + dot(qs[h, :, 640:768], states[h, 640:768, :])
        m = jnp.mean(a * a, axis=-1, keepdims=True)
        nrm[:, cols(h)] = (a * lax.rsqrt(m + EPS)).astype(BF)
        return 0

    lax.fori_loop(0, heads, norm_head, 0, unroll=True)
    cps[4].wait()

    top = tok // 2
    wide = out_ref.shape[1]
    tiles = mine.shape[1]
    tw = wide // tiles

    def tile_product(block, t):
        lo = pl.multiple_of(block * wide + t * tw, tw)
        return dot(nrm[...], w_v[:, pl.ds(lo, tw)])

    def y1(side, i):
        return pltpu.make_async_remote_copy(
            src_ref=p1s.at[side, i],
            dst_ref=p1r.at[side, i],
            send_sem=y1_s.at[side, i],
            recv_sem=y1_r.at[side, i],
            device_id=(p, (pa, pb)[side]),
            device_id_type=MESH,
        )

    def y2(side, i):
        return pltpu.make_async_remote_copy(
            src_ref=p2s.at[side, i],
            dst_ref=p2r.at[side, i],
            send_sem=y2_s.at[side, i],
            recv_sem=y2_r.at[side, i],
            device_id=(p, (pa, pb)[side]),
            device_id_type=MESH,
        )

    def far_tile(t, _):
        prod = tile_product(opp, t)
        p1s[0, t] = prod[:top].astype(BF)
        y1(0, t).start()
        p1s[1, t] = prod[top:].astype(BF)
        y1(1, t).start()
        return 0

    lax.fori_loop(0, tiles, far_tile, 0)

    def side_tile(t, _):
        prod = tile_product(pa, t)
        p1s[0, tiles + t] = prod[:top].astype(BF)
        y1(0, tiles + t).start()
        mine[0, t] = prod[top:]
        prod = tile_product(pb, t)
        p1s[1, tiles + t] = prod[top:].astype(BF)
        y1(1, tiles + t).start()
        mine[1, t] = prod[:top]
        return 0

    lax.fori_loop(0, tiles, side_tile, 0)

    def second(t, _):
        y1(1, t).wait_recv()
        p2s[0, t] = (mine[0, t] + p1r[1, t].astype(F32)).astype(BF)
        y2(0, t).start()
        y1(0, t).wait_recv()
        p2s[1, t] = (mine[1, t] + p1r[0, t].astype(F32)).astype(BF)
        y2(1, t).start()
        return 0

    def own_tile(t, _):
        own[t] = tile_product(y, t)
        return 0

    lax.fori_loop(0, tiles, own_tile, 0)
    lax.fori_loop(0, tiles, second, 0)

    def last(t, _):
        lanes = pl.ds(pl.multiple_of(t * tw, tw), tw)
        y1(0, tiles + t).wait_recv()
        y2(1, t).wait_recv()
        out_ref[pl.ds(0, top), lanes] = (
            own[t, pl.ds(0, top), :] + p1r[0, tiles + t].astype(F32) + p2r[1, t].astype(F32)
        ).astype(BF)
        y1(1, tiles + t).wait_recv()
        y2(0, t).wait_recv()
        out_ref[pl.ds(top, top), lanes] = (
            own[t, pl.ds(top, top), :] + p1r[1, tiles + t].astype(F32) + p2r[0, t].astype(F32)
        ).astype(BF)
        return 0

    lax.fori_loop(0, tiles, last, 0)

    for i in range(1, LINE):
        send1((d + i) % LINE).wait_send()

    @pl.when(core == 0)
    def _():
        core_copy.wait_send()

    for src in range(PLANES):

        @pl.when(z == src)
        def _():
            for slot, t in enumerate(TAKERS.get(src, ())):
                zcopy(slot, src, t).wait_send()
            for slot, t in enumerate(ROOTS.get(src, ())):
                zcopy(3 + slot, PLANES, t).wait_send()

    for c in range(1, CHIPS):

        @pl.when(x != c)
        def _():
            low_copy(c, c).wait_send()

        @pl.when(x == c)
        def _():
            low_copy(c, 0).wait_send()
            first = 0 if c % 2 else 1
            count = 2 if c == 3 else 1
            rows = pl.ds(128 + first * 128, count * 128)
            for i in range(1, CHIPS):
                spread(
                    states.at[0, rows, :], rows, mate, low_s, CHIPS + i - 1, low_r, 0
                ).wait_send()

    for cp in sends:
        cp.wait_send()
    for side in range(2):

        def drain(i, _):
            y1(side, i).wait_send()
            return 0

        lax.fori_loop(0, 2 * tiles, drain, 0)

        def drain2(i, _):
            y2(side, i).wait_send()
            return 0

        lax.fori_loop(0, tiles, drain2, 0)


def local(queries, keys, values, level_weights, out_weight):
    tok, width = queries.shape
    heads, levels, _ = level_weights.shape
    tiles = 4
    top = tok // 2
    tw = width // tiles
    dma = pltpu.SemaphoreType.DMA
    scratch = [
        pltpu.VMEM((tok, width), BF),
        pltpu.VMEM((tok, width), BF),
        pltpu.VMEM((tok, width), BF),
        pltpu.VMEM((levels, heads, tok), F32),
        pltpu.VMEM((tok, 128), F32),
        pltpu.VMEM(out_weight.shape, BF),
        pltpu.VMEM((heads, 3, 128, 128), BF),
        pltpu.VMEM((heads, 128, 128), BF),
        pltpu.VMEM((LINE, 128, 128), BF),
        pltpu.VMEM((CHIPS, 256, 128), BF),
        pltpu.VMEM((PLANES + 1, 128, 128), BF),
        pltpu.VMEM((heads, FAR * 128, 128), BF),
        pltpu.VMEM((heads, tok, FAR * 128), BF),
        pltpu.VMEM((tok, width), F32),
        pltpu.VMEM((tok, width), BF),
        pltpu.VMEM((2, 2 * tiles, top, tw), BF),
        pltpu.VMEM((2, 2 * tiles, top, tw), BF),
        pltpu.VMEM((2, tiles, top, tw), BF),
        pltpu.VMEM((2, tiles, top, tw), BF),
        pltpu.VMEM((2, tiles, top, tw), F32),
        pltpu.VMEM((tiles, tok, tw), F32),
        dma((5,)),
        dma((LINE,)),
        dma((LINE,)),
        dma,
        dma,
        dma((5,)),
        dma((PLANES + 1,)),
        dma((2 * CHIPS,)),
        dma((LINE,)),
        dma((2 * CHIPS,)),
        dma((LINE,)),
        dma((2 * CHIPS,)),
        dma((LINE,)),
        dma((2, 2 * tiles)),
        dma((2, 2 * tiles)),
        dma((2, tiles)),
        dma((2, tiles)),
    ]
    return pl.pallas_call(
        kernel,
        out_shape=pltpu.VMEM((tok, width), BF),
        in_specs=[pl.BlockSpec(memory_space=pl.ANY)] * 5,
        out_specs=pl.BlockSpec(memory_space=pltpu.VMEM),
        scratch_shapes=scratch,
        compiler_params=pltpu.CompilerParams(
            collective_id=0, has_side_effects=True, vmem_limit_bytes=60 * 1024 * 1024
        ),
    )(queries, keys, values, level_weights.transpose(1, 0, 2), out_weight)


def solution(mesh):
    in_specs = (
        P("seq", "head"),
        P("seq", "head"),
        P("seq", "head"),
        P("head", None, "seq"),
        P("head", None),
    )
    out_specs = P("seq", "head")
    return jax.shard_map(local, mesh=mesh, in_specs=in_specs, out_specs=out_specs, check_vma=False)
```

```python
import jax
import jax.numpy as jnp
from jax import lax
from jax.experimental import pallas as pl
from jax.experimental.pallas import tpu as pltpu
from jax.sharding import PartitionSpec as P

BLOCK = 128
EPS = 1e-06
LINE = 8
CHIPS = 4
PLANES = 8
FAR = 6
NEAR = (1, 2, 3, PLANES - 3, PLANES - 2, PLANES - 1)
TAKERS = {0: (3, 2, 1), 1: (3, 2, 0), 2: (3, 0), 3: (0,), 4: (7, 6, 5), 5: (7, 6), 6: (7,)}
ROOTS = {3: (5, 4), 0: (6, 7)}
BF = jnp.bfloat16
F32 = jnp.float32
MESH = pl.DeviceIdType.MESH


def dot(a, b):
    return jnp.dot(a, b, preferred_element_type=F32)


def kernel(
    q_hbm,
    k_hbm,
    v_hbm,
    lw_hbm,
    w_hbm,
    out_ref,
    q_v,
    k_v,
    v_v,
    lw_v,
    lw_t,
    w_v,
    bst,
    stbuf,
    recv1,
    lowbuf,
    zrecv,
    states,
    qs,
    tot,
    nrm,
    p1s,
    p1r,
    p2s,
    p2r,
    mine,
    own,
    wp,
    pn,
    h2s,
    h2r,
    ownh,
    in_sem,
    p1_s,
    p1_r,
    core_s,
    core_r,
    z_s,
    z_r,
    low_s,
    low_r,
    mid_s,
    mid_r,
    hi_s,
    hi_r,
    y1_s,
    y1_r,
    y2_s,
    y2_r,
    wf_s,
    w_s,
    w_r,
    hy_s,
    hy_r,
    h2_s,
    h2_r,
):
    heads = stbuf.shape[0]
    tok = q_v.shape[0]
    nblk = tok // BLOCK
    p = lax.axis_index("seq")
    y = lax.axis_index("head")
    z = p // LINE
    d = p % LINE
    core = d % 2
    x = d // 2
    pa = y + 1 - 2 * (y % 2)
    pb = 3 - y
    opp = (y + 2) % 4

    def line(e):
        return (z * LINE + e, y)

    def local_in(i, src, dst):
        return pltpu.make_async_copy(src, dst, in_sem.at[i])

    cps = [
        local_in(0, k_hbm, k_v),
        local_in(1, v_hbm, v_v),
        local_in(2, q_hbm, q_v),
        local_in(3, lw_hbm, lw_v),
        local_in(4, w_hbm, w_v),
    ]
    for c in cps:
        c.start()

    barrier = pltpu.get_barrier_semaphore()
    for i in range(1, LINE):
        pl.semaphore_signal(barrier, inc=1, device_id=line((d + i) % LINE), device_id_type=MESH)
    for i in NEAR:
        pl.semaphore_signal(
            barrier, inc=1, device_id=(((z + i) % PLANES) * LINE + d, y), device_id_type=MESH
        )
    for t in (pa, pb):
        pl.semaphore_signal(barrier, inc=1, device_id=(p, t), device_id_type=MESH)

    def cols(h):
        return pl.ds(pl.multiple_of(h * 128, 128), 128)

    @pl.when(core == 0)
    def _():
        states[:, pl.ds(0, 128), :] = jnp.zeros((heads, 128, 128), BF)

    @pl.when(x % 2 == 0)
    def _():
        states[:, pl.ds(128, 128), :] = jnp.zeros((heads, 128, 128), BF)

    @pl.when(x < 2)
    def _():
        states[:, pl.ds(256, 128), :] = jnp.zeros((heads, 128, 128), BF)

    cps[0].wait()
    cps[1].wait()

    def key_head(h, _):
        kf = k_v[:, cols(h)].astype(F32)
        ku = (kf * lax.rsqrt(jnp.sum(kf * kf, axis=-1, keepdims=True) + EPS)).astype(BF)
        k_v[:, cols(h)] = ku
        vv = v_v[:, cols(h)]
        s = [
            lax.dot_general(
                ku[b * BLOCK : (b + 1) * BLOCK],
                vv[b * BLOCK : (b + 1) * BLOCK],
                (((0,), (0,)), ((), ())),
                preferred_element_type=F32,
            )
            for b in range(nblk)
        ]
        s01 = s[0] + s[1]
        bst[h, 0] = s[0].astype(BF)
        bst[h, 1] = s[2].astype(BF)
        bst[h, 2] = s01.astype(BF)
        stbuf[h] = (s01 + s[2] + s[3]).astype(BF)
        return 0

    lax.fori_loop(0, heads, key_head, 0, unroll=True)
    pl.semaphore_wait(barrier, LINE - 1 + len(NEAR) + 2)

    def send1(e):
        return pltpu.make_async_remote_copy(
            src_ref=stbuf.at[e],
            dst_ref=recv1.at[d],
            send_sem=p1_s.at[e],
            recv_sem=p1_r.at[d],
            device_id=line(e),
            device_id_type=MESH,
        )

    for i in range(1, LINE):
        send1((d + i) % LINE).start()

    share = w_hbm.shape[0] // LINE
    width = out_ref.shape[1]
    my_rows = pl.ds(pl.multiple_of(d * share, share), share)

    def w_fetch(j):
        block = (pa, opp)[j]
        return pltpu.make_async_remote_copy(
            src_ref=w_hbm.at[my_rows, pl.ds(pl.multiple_of(block * width, width), width)],
            dst_ref=wp.at[j, my_rows, :],
            send_sem=wf_s.at[j],
            recv_sem=w_r.at[d, j],
            device_id=(p, pa),
            device_id_type=MESH,
        )

    for j in range(2):
        w_fetch(j).start()
    core_copy = pltpu.make_async_remote_copy(
        src_ref=stbuf,
        dst_ref=states.at[:, pl.ds(0, 128), :],
        send_sem=core_s,
        recv_sem=core_r,
        device_id=line(d + 1 - 2 * core),
        device_id_type=MESH,
    )

    @pl.when(core == 0)
    def _():
        core_copy.start()

    recv1[d] = stbuf[d]

    cps[2].wait()
    cps[3].wait()
    lw_all = lw_v[...].reshape(lw_v.shape[0] * heads, tok)
    lw_t[...] = jnp.concatenate([lw_all, jnp.zeros((128 - lw_all.shape[0], tok), F32)], axis=0).T

    def level_columns(h):
        return pltpu.roll(lw_t[...], lax.rem(128 - h, 128), 1)

    causal = lax.broadcasted_iota(jnp.int32, (BLOCK, BLOCK), 0) >= lax.broadcasted_iota(
        jnp.int32, (BLOCK, BLOCK), 1
    )

    def query_head(h, _):
        qf = q_v[:, cols(h)].astype(F32)
        qu = (qf * lax.rsqrt(jnp.sum(qf * qf, axis=-1, keepdims=True) + EPS)).astype(BF)
        q_v[:, cols(h)] = qu
        lwt = level_columns(h)
        for b in range(nblk):
            rows = pl.ds(b * BLOCK, BLOCK)
            part = slice(b * BLOCK, (b + 1) * BLOCK)
            qb = qu[part]
            s = lax.dot_general(
                qb, k_v[rows, cols(h)], (((1,), (1,)), ((), ())), preferred_element_type=F32
            )
            wgt = jnp.where(causal, s * lwt[part, 0:1], 0.0).astype(BF)
            acc = dot(wgt, v_v[rows, cols(h)])
            if b % 2 == 1:
                acc = acc + dot(qb, bst[h, b // 2]) * lwt[part, 8:9]
            if b >= 2:
                acc = acc + dot(qb, bst[h, 2]) * lwt[part, 16:17]
            tot[rows, cols(h)] = acc
        return 0

    lax.fori_loop(0, heads, query_head, 0, unroll=True)

    for i in range(1, LINE):
        e = (d + i) % LINE
        pltpu.make_async_remote_copy(
            src_ref=stbuf.at[e],
            dst_ref=recv1.at[e],
            send_sem=p1_s.at[e],
            recv_sem=p1_r.at[e],
            device_id=line(e),
            device_id_type=MESH,
        ).wait_recv()
    pair = [recv1[2 * c].astype(F32) + recv1[2 * c + 1].astype(F32) for c in range(CHIPS)]
    half = pair[0] + pair[1]
    zrecv[z] = (half + pair[2] + pair[3]).astype(BF)

    def zcopy(slot, src, t):
        return pltpu.make_async_remote_copy(
            src_ref=zrecv.at[src],
            dst_ref=zrecv.at[src],
            send_sem=z_s.at[slot],
            recv_sem=z_r.at[src],
            device_id=(t * LINE + d, y),
            device_id_type=MESH,
        )

    for src, takers in TAKERS.items():

        @pl.when(z == src)
        def _():
            for slot, t in enumerate(takers):
                zcopy(slot, src, t).start()

    none = jnp.zeros((128, 128), BF)
    for c in range(CHIPS):
        lowbuf[c, pl.ds(0, 128), :] = pair[c - 1].astype(BF) if c % 2 else none
        lowbuf[c, pl.ds(128, 128), :] = half.astype(BF) if c >= 2 else none

    mid_rows = pl.ds(384, 256)
    hi_rows = pl.ds(640, 128)

    def spread(src, rows, peer, s_sem, i, r_sem, h):
        return pltpu.make_async_remote_copy(
            src_ref=src,
            dst_ref=states.at[h, rows, :],
            send_sem=s_sem.at[i],
            recv_sem=r_sem.at[h],
            device_id=line(peer),
            device_id_type=MESH,
        )

    mate = d + 1 - 2 * core
    sends = []
    states[d, pl.ds(128, 256), :] = lowbuf[x]
    def low_copy(c, slot):
        first = 0 if c % 2 else 1
        count = 2 if c == 3 else 1
        return pltpu.make_async_remote_copy(
            src_ref=lowbuf.at[c, pl.ds(first * 128, count * 128), :],
            dst_ref=states.at[d, pl.ds(128 + first * 128, count * 128), :],
            send_sem=low_s.at[slot],
            recv_sem=low_r.at[d],
            device_id=line(mate if slot == 0 else c * 2 + core),
            device_id_type=MESH,
        )

    for c in range(1, CHIPS):

        @pl.when(x != c)
        def _():
            low_copy(c, c).start()

        @pl.when(x == c)
        def _():
            low_copy(c, 0).start()

    def scaled(h, levels):
        quf = q_v[:, cols(h)].astype(F32)
        lwt = level_columns(h)
        for lv in levels:
            col = 8 * (3 + lv)
            qs[h, :, lv * 128 : (lv + 1) * 128] = (quf * lwt[:, col : col + 1]).astype(BF)
        return 0

    def scale_low(h, _):
        return scaled(h, range(0, 3))

    def scale_high(h, _):
        return scaled(h, range(3, FAR))

    lax.fori_loop(0, heads, scale_low, 0, unroll=True)

    def low_forward(c):
        first = 0 if c % 2 else 1
        count = 2 if c == 3 else 1
        rows = pl.ds(128 + first * 128, count * 128)
        for i in range(1, CHIPS):
            h = ((c + i) % CHIPS) * 2 + core
            spread(states.at[h, rows, :], rows, mate, low_s, 0, low_r, h).wait_recv()
            spread(states.at[h, rows, :], rows, mate, low_s, CHIPS + i - 1, low_r, h).start()

    def low_landed(c):
        first = 0 if c % 2 else 1
        count = 2 if c == 3 else 1
        rows = pl.ds(128 + first * 128, count * 128)
        for i in range(CHIPS):
            h = i * 2 + 1 - core
            spread(states.at[h, rows, :], rows, mate, low_s, 0, low_r, h).wait_recv()

    def along_line(rows, s_sem, r_sem):
        src = states.at[d, rows, :]
        for i in (2, 1, 3, 0):
            e = ((x + i) % CHIPS) * 2 + core if i else mate
            cp = spread(src, rows, e, s_sem, i, r_sem, d)
            cp.start()
            sends.append(cp)

    def forward(rows, s_sem, r_sem):
        for i in (1, 3, 2):
            h = ((x + i) % CHIPS) * 2 + core
            src = states.at[h, rows, :]
            spread(src, rows, mate, s_sem, 0, r_sem, h).wait_recv()
            cp = spread(src, rows, mate, s_sem, 3 + i, r_sem, h)
            cp.start()
            sends.append(cp)

    def landed(rows, s_sem, r_sem):
        for i in range(CHIPS):
            h = i * 2 + 1 - core
            spread(states.at[h, rows, :], rows, mate, s_sem, 0, r_sem, h).wait_recv()

    for t in range(PLANES):

        @pl.when(z == t)
        def _():
            for src, takers in TAKERS.items():
                if t in takers:
                    zcopy(0, src, t).wait_recv()

    def put(row, val):
        states[d, pl.ds(row, 128), :] = val

    for root, takers in ROOTS.items():

        @pl.when(z == root)
        def _():
            q4 = [zrecv[i].astype(F32) for i in range(4)]
            zrecv[PLANES] = (q4[0] + q4[1] + q4[2] + q4[3]).astype(BF)
            for slot, t in enumerate(takers):
                zcopy(3 + slot, PLANES, t).start()

    base = (z // 4) * 4

    @pl.when(z % 2 == 1)
    def _():
        put(384, zrecv[z - 1])

    @pl.when(z % 2 == 0)
    def _():
        put(384, none)

    @pl.when((z // 2) % 2 == 1)
    def _():
        put(512, (zrecv[base].astype(F32) + zrecv[base + 1].astype(F32)).astype(BF))

    @pl.when((z // 2) % 2 == 0)
    def _():
        put(512, none)

    along_line(mid_rows, mid_s, mid_r)
    lax.fori_loop(0, heads, scale_high, 0, unroll=True)
    for c in range(1, CHIPS):

        @pl.when(x == c)
        def _():
            low_forward(c)

    @pl.when(z >= 4)
    def _():
        zcopy(0, PLANES, 0).wait_recv()
        put(640, zrecv[PLANES])

    @pl.when(z < 4)
    def _():
        put(640, none)

    along_line(hi_rows, hi_s, hi_r)
    for c in range(1, CHIPS):

        @pl.when(x == c)
        def _():
            low_landed(c)

    @pl.when(core == 1)
    def _():
        core_copy.wait_recv()

    def low_head(h, _):
        tot[:, cols(h)] += dot(qs[h, :, 0:384], states[h, 0:384, :])
        return 0

    lax.fori_loop(0, heads, low_head, 0, unroll=True)

    forward(mid_rows, mid_s, mid_r)
    landed(mid_rows, mid_s, mid_r)

    def mid_head(h, _):
        tot[:, cols(h)] += dot(qs[h, :, 384:640], states[h, 384:640, :])
        return 0

    ahead = (x + 1 + 2 * core) % CHIPS
    behind = (x + 3 - 2 * core) % CHIPS

    def w_move(h, j, peer, slot):
        rows = pl.ds(pl.multiple_of(h * share, share), share)
        return pltpu.make_async_remote_copy(
            src_ref=wp.at[j, rows, :],
            dst_ref=wp.at[j, rows, :],
            send_sem=w_s.at[slot, j],
            recv_sem=w_r.at[h, j],
            device_id=line(peer),
            device_id_type=MESH,
        )

    def w_send(h, j, peer, slot):
        cp = w_move(h, j, peer, slot)
        cp.start()
        sends.append(cp)

    for j in range(2):
        w_move(d, j, mate, 0).wait_recv()
        w_send(d, j, ahead * 2 + core, 0)
        w_send(d, j, behind * 2 + core, 1)
        w_send(d, j, mate, 2)

    lax.fori_loop(0, heads, mid_head, 0, unroll=True)

    forward(hi_rows, hi_s, hi_r)
    landed(hi_rows, hi_s, hi_r)

    def norm_head(h, _):
        a = tot[:, cols(h)] + dot(qs[h, :, 640:768], states[h, 640:768, :])
        m = jnp.mean(a * a, axis=-1, keepdims=True)
        nrm[:, cols(h)] = (a * lax.rsqrt(m + EPS)).astype(BF)
        return 0

    lax.fori_loop(0, heads, norm_head, 0, unroll=True)
    cps[4].wait()

    top = p1s.shape[2]
    lead = 2 * top
    tiles = mine.shape[1]
    tw = width // tiles

    def w_tile(block, t):
        return w_v[:, pl.ds(pl.multiple_of(block * width + t * tw, tw), tw)]

    def tile_product(block, t):
        return dot(nrm[pl.ds(0, lead), :], w_tile(block, t))

    def y1(side, i):
        return pltpu.make_async_remote_copy(
            src_ref=p1s.at[side, i],
            dst_ref=p1r.at[side, i],
            send_sem=y1_s.at[side, i],
            recv_sem=y1_r.at[side, i],
            device_id=(p, (pa, pb)[side]),
            device_id_type=MESH,
        )

    def y2(side, i):
        return pltpu.make_async_remote_copy(
            src_ref=p2s.at[side, i],
            dst_ref=p2r.at[side, i],
            send_sem=y2_s.at[side, i],
            recv_sem=y2_r.at[side, i],
            device_id=(p, (pa, pb)[side]),
            device_id_type=MESH,
        )

    def far_tile(t, _):
        prod = tile_product(opp, t)
        p1s[0, t] = prod[:top].astype(BF)
        y1(0, t).start()
        p1s[1, t] = prod[top:].astype(BF)
        y1(1, t).start()
        return 0

    lax.fori_loop(0, tiles, far_tile, 0)
    part = pn.shape[1]
    parts = pn.shape[0]

    def normed_copy(c):
        return pltpu.make_async_remote_copy(
            src_ref=nrm.at[pl.ds(lead + c * part, part), :],
            dst_ref=pn.at[c],
            send_sem=hy_s.at[c],
            recv_sem=hy_r.at[c],
            device_id=(p, pa),
            device_id_type=MESH,
        )

    for c in range(parts):
        normed_copy(c).start()

    def side_tile(t, _):
        prod = tile_product(pa, t)
        p1s[0, tiles + t] = prod[:top].astype(BF)
        y1(0, tiles + t).start()
        mine[0, t] = prod[top:]
        prod = tile_product(pb, t)
        p1s[1, tiles + t] = prod[top:].astype(BF)
        y1(1, tiles + t).start()
        mine[1, t] = prod[:top]
        return 0

    lax.fori_loop(0, tiles, side_tile, 0)

    def second(t, _):
        y1(1, t).wait_recv()
        p2s[0, t] = (mine[0, t] + p1r[1, t].astype(F32)).astype(BF)
        y2(0, t).start()
        y1(0, t).wait_recv()
        p2s[1, t] = (mine[1, t] + p1r[0, t].astype(F32)).astype(BF)
        y2(1, t).start()
        return 0

    def own_tile(t, _):
        own[t] = tile_product(y, t)
        return 0

    for j in range(2):
        h = behind * 2 + core
        w_move(h, j, mate, 0).wait_recv()
        w_send(h, j, ahead * 2 + core, 3)
        w_send(h, j, mate, 4)
    for j in range(2):
        h = ahead * 2 + core
        w_move(h, j, mate, 0).wait_recv()
        w_send(h, j, mate, 5)
    lax.fori_loop(0, tiles, own_tile, 0)
    lax.fori_loop(0, tiles, second, 0)
    for j in range(2):
        h = ((x + 2) % CHIPS) * 2 + core
        w_move(h, j, mate, 0).wait_recv()
        w_send(h, j, mate, 6)
    for j in range(2):
        for i in range(CHIPS):
            w_move(i * 2 + 1 - core, j, mate, 0).wait_recv()

    def h2(c, t):
        return pltpu.make_async_remote_copy(
            src_ref=h2s.at[c, t],
            dst_ref=h2r.at[c, t],
            send_sem=h2_s.at[c, t],
            recv_sem=h2_r.at[c, t],
            device_id=(p, pb),
            device_id_type=MESH,
        )

    def both(c, block, j, t):
        lanes = pl.ds(pl.multiple_of(t * tw, tw), tw)
        own_rows = nrm[pl.ds(lead + c * part, part), :]
        return dot(own_rows, w_tile(block, t)) + dot(pn[c], wp[j, :, lanes])

    for c in range(parts):
        normed_copy(c).wait_recv()

        def give_tile(t, _):
            h2s[c, t] = both(c, pb, 1, t).astype(BF)
            h2(c, t).start()
            return 0

        lax.fori_loop(0, tiles, give_tile, 0)

    for c in range(parts):

        def keep_tile(t, _):
            ownh[c, t] = both(c, y, 0, t)
            return 0

        lax.fori_loop(0, tiles, keep_tile, 0)

    def last(t, _):
        lanes = pl.ds(pl.multiple_of(t * tw, tw), tw)
        y1(0, tiles + t).wait_recv()
        y2(1, t).wait_recv()
        out_ref[pl.ds(0, top), lanes] = (
            own[t, pl.ds(0, top), :] + p1r[0, tiles + t].astype(F32) + p2r[1, t].astype(F32)
        ).astype(BF)
        y1(1, tiles + t).wait_recv()
        y2(0, t).wait_recv()
        out_ref[pl.ds(top, top), lanes] = (
            own[t, pl.ds(top, top), :] + p1r[1, tiles + t].astype(F32) + p2r[0, t].astype(F32)
        ).astype(BF)
        return 0

    lax.fori_loop(0, tiles, last, 0)
    for c in range(parts):

        def last_given(t, _):
            lanes = pl.ds(pl.multiple_of(t * tw, tw), tw)
            h2(c, t).wait_recv()
            out_ref[pl.ds(lead + c * part, part), lanes] = (
                ownh[c, t] + h2r[c, t].astype(F32)
            ).astype(BF)
            return 0

        lax.fori_loop(0, tiles, last_given, 0)

    for j in range(2):
        w_fetch(j).wait_send()
    for c in range(parts):
        normed_copy(c).wait_send()

        def drain3(t, _):
            h2(c, t).wait_send()
            return 0

        lax.fori_loop(0, tiles, drain3, 0)

    for i in range(1, LINE):
        send1((d + i) % LINE).wait_send()

    @pl.when(core == 0)
    def _():
        core_copy.wait_send()

    for src in range(PLANES):

        @pl.when(z == src)
        def _():
            for slot, t in enumerate(TAKERS.get(src, ())):
                zcopy(slot, src, t).wait_send()
            for slot, t in enumerate(ROOTS.get(src, ())):
                zcopy(3 + slot, PLANES, t).wait_send()

    for c in range(1, CHIPS):

        @pl.when(x != c)
        def _():
            low_copy(c, c).wait_send()

        @pl.when(x == c)
        def _():
            low_copy(c, 0).wait_send()
            first = 0 if c % 2 else 1
            count = 2 if c == 3 else 1
            rows = pl.ds(128 + first * 128, count * 128)
            for i in range(1, CHIPS):
                spread(
                    states.at[0, rows, :], rows, mate, low_s, CHIPS + i - 1, low_r, 0
                ).wait_send()

    for cp in sends:
        cp.wait_send()
    for side in range(2):

        def drain(i, _):
            y1(side, i).wait_send()
            return 0

        lax.fori_loop(0, 2 * tiles, drain, 0)

        def drain2(i, _):
            y2(side, i).wait_send()
            return 0

        lax.fori_loop(0, tiles, drain2, 0)


def local(queries, keys, values, level_weights, out_weight):
    tok, width = queries.shape
    heads, levels, _ = level_weights.shape
    tiles = 4
    top = tok // 4
    parts = 2
    part = (tok - 2 * top) // parts
    tw = width // tiles
    dma = pltpu.SemaphoreType.DMA
    scratch = [
        pltpu.VMEM((tok, width), BF),
        pltpu.VMEM((tok, width), BF),
        pltpu.VMEM((tok, width), BF),
        pltpu.VMEM((levels, heads, tok), F32),
        pltpu.VMEM((tok, 128), F32),
        pltpu.VMEM(out_weight.shape, BF),
        pltpu.VMEM((heads, 3, 128, 128), BF),
        pltpu.VMEM((heads, 128, 128), BF),
        pltpu.VMEM((LINE, 128, 128), BF),
        pltpu.VMEM((CHIPS, 256, 128), BF),
        pltpu.VMEM((PLANES + 1, 128, 128), BF),
        pltpu.VMEM((heads, FAR * 128, 128), BF),
        pltpu.VMEM((heads, tok, FAR * 128), BF),
        pltpu.VMEM((tok, width), F32),
        pltpu.VMEM((tok, width), BF),
        pltpu.VMEM((2, 2 * tiles, top, tw), BF),
        pltpu.VMEM((2, 2 * tiles, top, tw), BF),
        pltpu.VMEM((2, tiles, top, tw), BF),
        pltpu.VMEM((2, tiles, top, tw), BF),
        pltpu.VMEM((2, tiles, top, tw), F32),
        pltpu.VMEM((tiles, 2 * top, tw), F32),
        pltpu.VMEM((2, width, width), BF),
        pltpu.VMEM((parts, part, width), BF),
        pltpu.VMEM((parts, tiles, part, tw), BF),
        pltpu.VMEM((parts, tiles, part, tw), BF),
        pltpu.VMEM((parts, tiles, part, tw), F32),
        dma((5,)),
        dma((LINE,)),
        dma((LINE,)),
        dma,
        dma,
        dma((5,)),
        dma((PLANES + 1,)),
        dma((2 * CHIPS,)),
        dma((LINE,)),
        dma((2 * CHIPS,)),
        dma((LINE,)),
        dma((2 * CHIPS,)),
        dma((LINE,)),
        dma((2, 2 * tiles)),
        dma((2, 2 * tiles)),
        dma((2, tiles)),
        dma((2, tiles)),
        dma((2,)),
        dma((7, 2)),
        dma((LINE, 2)),
        dma((parts,)),
        dma((parts,)),
        dma((parts, tiles)),
        dma((parts, tiles)),
    ]
    return pl.pallas_call(
        kernel,
        out_shape=pltpu.VMEM((tok, width), BF),
        in_specs=[pl.BlockSpec(memory_space=pl.ANY)] * 5,
        out_specs=pl.BlockSpec(memory_space=pltpu.VMEM),
        scratch_shapes=scratch,
        compiler_params=pltpu.CompilerParams(
            collective_id=0, has_side_effects=True, vmem_limit_bytes=60 * 1024 * 1024
        ),
    )(queries, keys, values, level_weights.transpose(1, 0, 2), out_weight)


def solution(mesh):
    in_specs = (
        P("seq", "head"),
        P("seq", "head"),
        P("seq", "head"),
        P("head", None, "seq"),
        P("head", None),
    )
    out_specs = P("seq", "head")
    return jax.shard_map(local, mesh=mesh, in_specs=in_specs, out_specs=out_specs, check_vma=False)
```

```python
import jax
import jax.numpy as jnp
from jax import lax
from jax.experimental import pallas as pl
from jax.experimental.pallas import tpu as pltpu
from jax.sharding import PartitionSpec as P

BLOCK = 128
EPS = 1e-06
LINE = 8
CHIPS = 4
PLANES = 8
FAR = 6
DIRECT = 256
NEAR = (1, 2, 3, PLANES - 3, PLANES - 2, PLANES - 1)
TAKERS = {0: (3, 2, 1), 1: (3, 2, 0), 2: (3, 0), 3: (0,), 4: (7, 6, 5), 5: (7, 6), 6: (7,)}
ROOTS = {3: (5, 4), 0: (6, 7)}
BF = jnp.bfloat16
F32 = jnp.float32
MESH = pl.DeviceIdType.MESH


def dot(a, b):
    return jnp.dot(a, b, preferred_element_type=F32)


def kernel(
    q_hbm,
    k_hbm,
    v_hbm,
    lw_hbm,
    w_hbm,
    out_ref,
    q_v,
    k_v,
    v_v,
    lw_v,
    lw_t,
    w_v,
    bst,
    stbuf,
    recv1,
    lowbuf,
    zrecv,
    states,
    qs,
    tot,
    nrm,
    p1s,
    p1r,
    p2s,
    p2r,
    mine,
    own,
    wp,
    pn,
    h2s,
    h2r,
    ownh,
    in_sem,
    p1_s,
    p1_r,
    core_s,
    core_r,
    z_s,
    z_r,
    low_s,
    low_r,
    mid_s,
    mid_r,
    hi_s,
    hi_r,
    y1_s,
    y1_r,
    y2_s,
    y2_r,
    wf_s,
    w_s,
    w_r,
    hy_s,
    hy_r,
    h2_s,
    h2_r,
):
    heads = stbuf.shape[0]
    tok = q_v.shape[0]
    nblk = tok // BLOCK
    p = lax.axis_index("seq")
    y = lax.axis_index("head")
    z = p // LINE
    d = p % LINE
    core = d % 2
    x = d // 2
    pa = y + 1 - 2 * (y % 2)
    pb = 3 - y
    opp = (y + 2) % 4

    def line(e):
        return (z * LINE + e, y)

    def local_in(i, src, dst):
        return pltpu.make_async_copy(src, dst, in_sem.at[i])

    cps = [
        local_in(0, k_hbm, k_v),
        local_in(1, v_hbm, v_v),
        local_in(2, q_hbm, q_v),
        local_in(3, lw_hbm, lw_v),
        local_in(4, w_hbm, w_v),
    ]
    for c in cps:
        c.start()

    barrier = pltpu.get_barrier_semaphore()
    for i in range(1, LINE):
        pl.semaphore_signal(barrier, inc=1, device_id=line((d + i) % LINE), device_id_type=MESH)
    for i in NEAR:
        pl.semaphore_signal(
            barrier, inc=1, device_id=(((z + i) % PLANES) * LINE + d, y), device_id_type=MESH
        )
    for t in (pa, pb):
        pl.semaphore_signal(barrier, inc=1, device_id=(p, t), device_id_type=MESH)

    def cols(h):
        return pl.ds(pl.multiple_of(h * 128, 128), 128)

    @pl.when(core == 0)
    def _():
        states[:, pl.ds(0, 128), :] = jnp.zeros((heads, 128, 128), BF)

    @pl.when(x % 2 == 0)
    def _():
        states[:, pl.ds(128, 128), :] = jnp.zeros((heads, 128, 128), BF)

    @pl.when(x < 2)
    def _():
        states[:, pl.ds(256, 128), :] = jnp.zeros((heads, 128, 128), BF)

    cps[0].wait()
    cps[1].wait()

    def key_head(h, _):
        kf = k_v[:, cols(h)].astype(F32)
        ku = (kf * lax.rsqrt(jnp.sum(kf * kf, axis=-1, keepdims=True) + EPS)).astype(BF)
        k_v[:, cols(h)] = ku
        vv = v_v[:, cols(h)]
        s = [
            lax.dot_general(
                ku[b * BLOCK : (b + 1) * BLOCK],
                vv[b * BLOCK : (b + 1) * BLOCK],
                (((0,), (0,)), ((), ())),
                preferred_element_type=F32,
            )
            for b in range(nblk)
        ]
        s01 = s[0] + s[1]
        bst[h, 0] = s[0].astype(BF)
        bst[h, 1] = s[2].astype(BF)
        bst[h, 2] = s01.astype(BF)
        stbuf[h] = (s01 + s[2] + s[3]).astype(BF)
        return 0

    lax.fori_loop(0, heads, key_head, 0, unroll=True)
    pl.semaphore_wait(barrier, LINE - 1 + len(NEAR) + 2)

    def send1(e):
        return pltpu.make_async_remote_copy(
            src_ref=stbuf.at[e],
            dst_ref=recv1.at[d],
            send_sem=p1_s.at[e],
            recv_sem=p1_r.at[d],
            device_id=line(e),
            device_id_type=MESH,
        )

    for i in (2, 1, 3):
        for c in range(2):
            send1(((x + i) % CHIPS) * 2 + c).start()
    send1(d + 1 - 2 * core).start()

    share = (w_hbm.shape[0] - DIRECT) // LINE
    width = out_ref.shape[1]

    def w_rows(h):
        return pl.ds(pl.multiple_of(DIRECT + h * share, 16), share)

    def chip_rows(c):
        return pl.ds(pl.multiple_of(c * (DIRECT // 2), 16), DIRECT // 2)

    def w_fetch(i):
        j = i % 2
        block = (pa, opp)[j]
        rows, piece = (w_rows(d), d) if i < 2 else (chip_rows(core), LINE + core)
        return pltpu.make_async_remote_copy(
            src_ref=w_hbm.at[rows, pl.ds(pl.multiple_of(block * width, width), width)],
            dst_ref=wp.at[j, rows, :],
            send_sem=wf_s.at[i],
            recv_sem=w_r.at[piece, j],
            device_id=(p, pa),
            device_id_type=MESH,
        )

    fetches = 4 if DIRECT else 2
    for i in range(fetches):
        w_fetch(i).start()
    core_copy = pltpu.make_async_remote_copy(
        src_ref=stbuf,
        dst_ref=states.at[:, pl.ds(0, 128), :],
        send_sem=core_s,
        recv_sem=core_r,
        device_id=line(d + 1 - 2 * core),
        device_id_type=MESH,
    )

    @pl.when(core == 0)
    def _():
        core_copy.start()

    recv1[d] = stbuf[d]

    cps[2].wait()
    cps[3].wait()
    lw_all = lw_v[...].reshape(lw_v.shape[0] * heads, tok)
    lw_t[...] = jnp.concatenate([lw_all, jnp.zeros((128 - lw_all.shape[0], tok), F32)], axis=0).T

    def level_columns(h):
        return pltpu.roll(lw_t[...], lax.rem(128 - h, 128), 1)

    causal = lax.broadcasted_iota(jnp.int32, (BLOCK, BLOCK), 0) >= lax.broadcasted_iota(
        jnp.int32, (BLOCK, BLOCK), 1
    )

    def query_head(h, _):
        qf = q_v[:, cols(h)].astype(F32)
        qu = (qf * lax.rsqrt(jnp.sum(qf * qf, axis=-1, keepdims=True) + EPS)).astype(BF)
        q_v[:, cols(h)] = qu
        lwt = level_columns(h)
        for b in range(nblk):
            rows = pl.ds(b * BLOCK, BLOCK)
            part = slice(b * BLOCK, (b + 1) * BLOCK)
            qb = qu[part]
            s = lax.dot_general(
                qb, k_v[rows, cols(h)], (((1,), (1,)), ((), ())), preferred_element_type=F32
            )
            wgt = jnp.where(causal, s * lwt[part, 0:1], 0.0).astype(BF)
            acc = dot(wgt, v_v[rows, cols(h)])
            if b % 2 == 1:
                acc = acc + dot(qb, bst[h, b // 2]) * lwt[part, 8:9]
            if b >= 2:
                acc = acc + dot(qb, bst[h, 2]) * lwt[part, 16:17]
            tot[rows, cols(h)] = acc
        return 0

    lax.fori_loop(0, heads, query_head, 0, unroll=True)

    for i in range(1, LINE):
        e = (d + i) % LINE
        pltpu.make_async_remote_copy(
            src_ref=stbuf.at[e],
            dst_ref=recv1.at[e],
            send_sem=p1_s.at[e],
            recv_sem=p1_r.at[e],
            device_id=line(e),
            device_id_type=MESH,
        ).wait_recv()
    pair = [recv1[2 * c].astype(F32) + recv1[2 * c + 1].astype(F32) for c in range(CHIPS)]
    half = pair[0] + pair[1]
    zrecv[z] = (half + pair[2] + pair[3]).astype(BF)

    def zcopy(slot, src, t):
        return pltpu.make_async_remote_copy(
            src_ref=zrecv.at[src],
            dst_ref=zrecv.at[src],
            send_sem=z_s.at[slot],
            recv_sem=z_r.at[src],
            device_id=(t * LINE + d, y),
            device_id_type=MESH,
        )

    for src, takers in TAKERS.items():

        @pl.when(z == src)
        def _():
            for slot, t in enumerate(takers):
                zcopy(slot, src, t).start()

    none = jnp.zeros((128, 128), BF)
    for c in range(CHIPS):
        lowbuf[c, pl.ds(0, 128), :] = pair[c - 1].astype(BF) if c % 2 else none
        lowbuf[c, pl.ds(128, 128), :] = half.astype(BF) if c >= 2 else none

    mid_rows = pl.ds(384, 256)
    hi_rows = pl.ds(640, 128)

    def spread(src, rows, peer, s_sem, i, r_sem, h):
        return pltpu.make_async_remote_copy(
            src_ref=src,
            dst_ref=states.at[h, rows, :],
            send_sem=s_sem.at[i],
            recv_sem=r_sem.at[h],
            device_id=line(peer),
            device_id_type=MESH,
        )

    mate = d + 1 - 2 * core
    sends = []
    states[d, pl.ds(128, 256), :] = lowbuf[x]
    def low_copy(c, slot):
        first = 0 if c % 2 else 1
        count = 2 if c == 3 else 1
        return pltpu.make_async_remote_copy(
            src_ref=lowbuf.at[c, pl.ds(first * 128, count * 128), :],
            dst_ref=states.at[d, pl.ds(128 + first * 128, count * 128), :],
            send_sem=low_s.at[slot],
            recv_sem=low_r.at[d],
            device_id=line(mate if slot == 0 else c * 2 + core),
            device_id_type=MESH,
        )

    for c in range(1, CHIPS):

        @pl.when(x != c)
        def _():
            low_copy(c, c).start()

        @pl.when(x == c)
        def _():
            low_copy(c, 0).start()

    def scaled(h, levels):
        quf = q_v[:, cols(h)].astype(F32)
        lwt = level_columns(h)
        for lv in levels:
            col = 8 * (3 + lv)
            qs[h, :, lv * 128 : (lv + 1) * 128] = (quf * lwt[:, col : col + 1]).astype(BF)
        return 0

    def scale_low(h, _):
        return scaled(h, range(0, 3))

    def scale_high(h, _):
        return scaled(h, range(3, FAR))

    lax.fori_loop(0, heads, scale_low, 0, unroll=True)

    def low_forward(c):
        first = 0 if c % 2 else 1
        count = 2 if c == 3 else 1
        rows = pl.ds(128 + first * 128, count * 128)
        for i in range(1, CHIPS):
            h = ((c + i) % CHIPS) * 2 + core
            spread(states.at[h, rows, :], rows, mate, low_s, 0, low_r, h).wait_recv()
            spread(states.at[h, rows, :], rows, mate, low_s, CHIPS + i - 1, low_r, h).start()

    def low_landed(c):
        first = 0 if c % 2 else 1
        count = 2 if c == 3 else 1
        rows = pl.ds(128 + first * 128, count * 128)
        for i in range(CHIPS):
            h = i * 2 + 1 - core
            spread(states.at[h, rows, :], rows, mate, low_s, 0, low_r, h).wait_recv()

    def along_line(rows, s_sem, r_sem):
        src = states.at[d, rows, :]
        for i in (2, 1, 3, 0):
            e = ((x + i) % CHIPS) * 2 + core if i else mate
            cp = spread(src, rows, e, s_sem, i, r_sem, d)
            cp.start()
            sends.append(cp)

    def forward(rows, s_sem, r_sem):
        for i in (1, 3, 2):
            h = ((x + i) % CHIPS) * 2 + core
            src = states.at[h, rows, :]
            spread(src, rows, mate, s_sem, 0, r_sem, h).wait_recv()
            cp = spread(src, rows, mate, s_sem, 3 + i, r_sem, h)
            cp.start()
            sends.append(cp)

    def landed(rows, s_sem, r_sem):
        for i in range(CHIPS):
            h = i * 2 + 1 - core
            spread(states.at[h, rows, :], rows, mate, s_sem, 0, r_sem, h).wait_recv()

    for t in range(PLANES):

        @pl.when(z == t)
        def _():
            for src, takers in TAKERS.items():
                if t in takers:
                    zcopy(0, src, t).wait_recv()

    def put(row, val):
        states[d, pl.ds(row, 128), :] = val

    for root, takers in ROOTS.items():

        @pl.when(z == root)
        def _():
            q4 = [zrecv[i].astype(F32) for i in range(4)]
            zrecv[PLANES] = (q4[0] + q4[1] + q4[2] + q4[3]).astype(BF)
            for slot, t in enumerate(takers):
                zcopy(3 + slot, PLANES, t).start()

    base = (z // 4) * 4

    @pl.when(z % 2 == 1)
    def _():
        put(384, zrecv[z - 1])

    @pl.when(z % 2 == 0)
    def _():
        put(384, none)

    @pl.when((z // 2) % 2 == 1)
    def _():
        put(512, (zrecv[base].astype(F32) + zrecv[base + 1].astype(F32)).astype(BF))

    @pl.when((z // 2) % 2 == 0)
    def _():
        put(512, none)

    along_line(mid_rows, mid_s, mid_r)
    lax.fori_loop(0, heads, scale_high, 0, unroll=True)
    for c in range(1, CHIPS):

        @pl.when(x == c)
        def _():
            low_forward(c)

    @pl.when(z >= 4)
    def _():
        zcopy(0, PLANES, 0).wait_recv()
        put(640, zrecv[PLANES])

    @pl.when(z < 4)
    def _():
        put(640, none)

    along_line(hi_rows, hi_s, hi_r)
    for c in range(1, CHIPS):

        @pl.when(x == c)
        def _():
            low_landed(c)

    @pl.when(core == 1)
    def _():
        core_copy.wait_recv()

    def low_head(h, _):
        tot[:, cols(h)] += dot(qs[h, :, 0:384], states[h, 0:384, :])
        return 0

    lax.fori_loop(0, heads, low_head, 0, unroll=True)

    forward(mid_rows, mid_s, mid_r)
    landed(mid_rows, mid_s, mid_r)

    def mid_head(h, _):
        tot[:, cols(h)] += dot(qs[h, :, 384:640], states[h, 384:640, :])
        return 0

    ahead = (x + 1 + 2 * core) % CHIPS
    behind = (x + 3 - 2 * core) % CHIPS

    def w_move(h, j, peer, slot, rows=None):
        rows = w_rows(h) if rows is None else rows
        return pltpu.make_async_remote_copy(
            src_ref=wp.at[j, rows, :],
            dst_ref=wp.at[j, rows, :],
            send_sem=w_s.at[slot, j],
            recv_sem=w_r.at[h, j],
            device_id=line(peer),
            device_id_type=MESH,
        )

    def w_send(h, j, peer, slot):
        cp = w_move(h, j, peer, slot)
        cp.start()
        sends.append(cp)

    for j in range(2):
        w_move(d, j, mate, 0).wait_recv()
        w_send(d, j, ahead * 2 + core, 0)
        w_send(d, j, behind * 2 + core, 1)
        w_send(d, j, mate, 2)

    forward(hi_rows, hi_s, hi_r)
    lax.fori_loop(0, heads, mid_head, 0, unroll=True)

    landed(hi_rows, hi_s, hi_r)

    top = p1s.shape[2]
    lead = 2 * top

    def normalize(lo, n):
        rows = pl.ds(lo, n)

        def norm_head(h, _):
            a = tot[rows, cols(h)] + dot(qs[h, rows, 640:768], states[h, 640:768, :])
            m = jnp.mean(a * a, axis=-1, keepdims=True)
            nrm[rows, cols(h)] = (a * lax.rsqrt(m + EPS)).astype(BF)
            return 0

        lax.fori_loop(0, heads, norm_head, 0, unroll=True)

    normalize(0, lead)
    cps[4].wait()

    tiles = mine.shape[1]
    tw = width // tiles

    def w_tile(block, t):
        return w_v[:, pl.ds(pl.multiple_of(block * width + t * tw, tw), tw)]

    def tile_product(block, t):
        return dot(nrm[pl.ds(0, lead), :], w_tile(block, t))

    def y1(side, i):
        return pltpu.make_async_remote_copy(
            src_ref=p1s.at[side, i],
            dst_ref=p1r.at[side, i],
            send_sem=y1_s.at[side, i],
            recv_sem=y1_r.at[side, i],
            device_id=(p, (pa, pb)[side]),
            device_id_type=MESH,
        )

    def y2(side, i):
        return pltpu.make_async_remote_copy(
            src_ref=p2s.at[side, i],
            dst_ref=p2r.at[side, i],
            send_sem=y2_s.at[side, i],
            recv_sem=y2_r.at[side, i],
            device_id=(p, (pa, pb)[side]),
            device_id_type=MESH,
        )

    def far_tile(t, _):
        prod = tile_product(opp, t)
        p1s[0, t] = prod[:top].astype(BF)
        y1(0, t).start()
        p1s[1, t] = prod[top:].astype(BF)
        y1(1, t).start()
        return 0

    lax.fori_loop(0, tiles, far_tile, 0)
    part = pn.shape[1]
    parts = pn.shape[0]

    def normed_copy(c):
        return pltpu.make_async_remote_copy(
            src_ref=nrm.at[pl.ds(lead + c * part, part), :],
            dst_ref=pn.at[c],
            send_sem=hy_s.at[c],
            recv_sem=hy_r.at[c],
            device_id=(p, pa),
            device_id_type=MESH,
        )

    for c in range(parts):
        normalize(lead + c * part, part)
        normed_copy(c).start()

    def side_tile(t, _):
        prod = tile_product(pa, t)
        p1s[0, tiles + t] = prod[:top].astype(BF)
        y1(0, tiles + t).start()
        mine[0, t] = prod[top:]
        prod = tile_product(pb, t)
        p1s[1, tiles + t] = prod[top:].astype(BF)
        y1(1, tiles + t).start()
        mine[1, t] = prod[:top]
        return 0

    lax.fori_loop(0, tiles, side_tile, 0)

    def second(t, _):
        y1(1, t).wait_recv()
        p2s[0, t] = (mine[0, t] + p1r[1, t].astype(F32)).astype(BF)
        y2(0, t).start()
        y1(0, t).wait_recv()
        p2s[1, t] = (mine[1, t] + p1r[0, t].astype(F32)).astype(BF)
        y2(1, t).start()
        return 0

    def own_tile(t, _):
        own[t] = tile_product(y, t)
        return 0

    if DIRECT:
        for j in range(2):
            w_move(LINE + core, j, mate, 7, chip_rows(core)).wait_recv()
            cp = w_move(LINE + core, j, mate, 7, chip_rows(core))
            cp.start()
            sends.append(cp)
    for j in range(2):
        h = behind * 2 + core
        w_move(h, j, mate, 0).wait_recv()
        w_send(h, j, ahead * 2 + core, 3)
        w_send(h, j, mate, 4)
    for j in range(2):
        h = ahead * 2 + core
        w_move(h, j, mate, 0).wait_recv()
        w_send(h, j, mate, 5)
    lax.fori_loop(0, tiles, own_tile, 0)
    lax.fori_loop(0, tiles, second, 0)
    for j in range(2):
        h = ((x + 2) % CHIPS) * 2 + core
        w_move(h, j, mate, 0).wait_recv()
        w_send(h, j, mate, 6)
    for j in range(2):
        for i in range(CHIPS):
            w_move(i * 2 + 1 - core, j, mate, 0).wait_recv()
        if DIRECT:
            w_move(LINE + 1 - core, j, mate, 0, chip_rows(1 - core)).wait_recv()

    def h2(c, t):
        return pltpu.make_async_remote_copy(
            src_ref=h2s.at[c, t],
            dst_ref=h2r.at[c, t],
            send_sem=h2_s.at[c, t],
            recv_sem=h2_r.at[c, t],
            device_id=(p, pb),
            device_id_type=MESH,
        )

    def both(c, block, j, t):
        lanes = pl.ds(pl.multiple_of(t * tw, tw), tw)
        own_rows = nrm[pl.ds(lead + c * part, part), :]
        return dot(own_rows, w_tile(block, t)) + dot(pn[c], wp[j, :, lanes])

    for c in range(parts):
        normed_copy(c).wait_recv()

        def give_tile(t, _):
            h2s[c, t] = both(c, pb, 1, t).astype(BF)
            h2(c, t).start()
            return 0

        lax.fori_loop(0, tiles, give_tile, 0)

    for c in range(parts):

        def keep_tile(t, _):
            ownh[c, t] = both(c, y, 0, t)
            return 0

        lax.fori_loop(0, tiles, keep_tile, 0)

    def last(t, _):
        lanes = pl.ds(pl.multiple_of(t * tw, tw), tw)
        y1(0, tiles + t).wait_recv()
        y2(1, t).wait_recv()
        out_ref[pl.ds(0, top), lanes] = (
            own[t, pl.ds(0, top), :] + p1r[0, tiles + t].astype(F32) + p2r[1, t].astype(F32)
        ).astype(BF)
        y1(1, tiles + t).wait_recv()
        y2(0, t).wait_recv()
        out_ref[pl.ds(top, top), lanes] = (
            own[t, pl.ds(top, top), :] + p1r[1, tiles + t].astype(F32) + p2r[0, t].astype(F32)
        ).astype(BF)
        return 0

    lax.fori_loop(0, tiles, last, 0)
    for c in range(parts):

        def last_given(t, _):
            lanes = pl.ds(pl.multiple_of(t * tw, tw), tw)
            h2(c, t).wait_recv()
            out_ref[pl.ds(lead + c * part, part), lanes] = (
                ownh[c, t] + h2r[c, t].astype(F32)
            ).astype(BF)
            return 0

        lax.fori_loop(0, tiles, last_given, 0)

    for i in range(fetches):
        w_fetch(i).wait_send()
    for c in range(parts):
        normed_copy(c).wait_send()

        def drain3(t, _):
            h2(c, t).wait_send()
            return 0

        lax.fori_loop(0, tiles, drain3, 0)

    for i in range(1, LINE):
        send1((d + i) % LINE).wait_send()

    @pl.when(core == 0)
    def _():
        core_copy.wait_send()

    for src in range(PLANES):

        @pl.when(z == src)
        def _():
            for slot, t in enumerate(TAKERS.get(src, ())):
                zcopy(slot, src, t).wait_send()
            for slot, t in enumerate(ROOTS.get(src, ())):
                zcopy(3 + slot, PLANES, t).wait_send()

    for c in range(1, CHIPS):

        @pl.when(x != c)
        def _():
            low_copy(c, c).wait_send()

        @pl.when(x == c)
        def _():
            low_copy(c, 0).wait_send()
            first = 0 if c % 2 else 1
            count = 2 if c == 3 else 1
            rows = pl.ds(128 + first * 128, count * 128)
            for i in range(1, CHIPS):
                spread(
                    states.at[0, rows, :], rows, mate, low_s, CHIPS + i - 1, low_r, 0
                ).wait_send()

    for cp in sends:
        cp.wait_send()
    for side in range(2):

        def drain(i, _):
            y1(side, i).wait_send()
            return 0

        lax.fori_loop(0, 2 * tiles, drain, 0)

        def drain2(i, _):
            y2(side, i).wait_send()
            return 0

        lax.fori_loop(0, tiles, drain2, 0)


def local(queries, keys, values, level_weights, out_weight):
    tok, width = queries.shape
    heads, levels, _ = level_weights.shape
    tiles = 4
    top = 96
    parts = 2
    part = (tok - 2 * top) // parts
    tw = width // tiles
    dma = pltpu.SemaphoreType.DMA
    scratch = [
        pltpu.VMEM((tok, width), BF),
        pltpu.VMEM((tok, width), BF),
        pltpu.VMEM((tok, width), BF),
        pltpu.VMEM((levels, heads, tok), F32),
        pltpu.VMEM((tok, 128), F32),
        pltpu.VMEM(out_weight.shape, BF),
        pltpu.VMEM((heads, 3, 128, 128), BF),
        pltpu.VMEM((heads, 128, 128), BF),
        pltpu.VMEM((LINE, 128, 128), BF),
        pltpu.VMEM((CHIPS, 256, 128), BF),
        pltpu.VMEM((PLANES + 1, 128, 128), BF),
        pltpu.VMEM((heads, FAR * 128, 128), BF),
        pltpu.VMEM((heads, tok, FAR * 128), BF),
        pltpu.VMEM((tok, width), F32),
        pltpu.VMEM((tok, width), BF),
        pltpu.VMEM((2, 2 * tiles, top, tw), BF),
        pltpu.VMEM((2, 2 * tiles, top, tw), BF),
        pltpu.VMEM((2, tiles, top, tw), BF),
        pltpu.VMEM((2, tiles, top, tw), BF),
        pltpu.VMEM((2, tiles, top, tw), F32),
        pltpu.VMEM((tiles, 2 * top, tw), F32),
        pltpu.VMEM((2, width, width), BF),
        pltpu.VMEM((parts, part, width), BF),
        pltpu.VMEM((parts, tiles, part, tw), BF),
        pltpu.VMEM((parts, tiles, part, tw), BF),
        pltpu.VMEM((parts, tiles, part, tw), F32),
        dma((5,)),
        dma((LINE,)),
        dma((LINE,)),
        dma,
        dma,
        dma((5,)),
        dma((PLANES + 1,)),
        dma((2 * CHIPS,)),
        dma((LINE,)),
        dma((2 * CHIPS,)),
        dma((LINE,)),
        dma((2 * CHIPS,)),
        dma((LINE,)),
        dma((2, 2 * tiles)),
        dma((2, 2 * tiles)),
        dma((2, tiles)),
        dma((2, tiles)),
        dma((4,)),
        dma((8, 2)),
        dma((LINE + 2, 2)),
        dma((parts,)),
        dma((parts,)),
        dma((parts, tiles)),
        dma((parts, tiles)),
    ]
    return pl.pallas_call(
        kernel,
        out_shape=pltpu.VMEM((tok, width), BF),
        in_specs=[pl.BlockSpec(memory_space=pl.ANY)] * 5,
        out_specs=pl.BlockSpec(memory_space=pltpu.VMEM),
        scratch_shapes=scratch,
        compiler_params=pltpu.CompilerParams(
            collective_id=0, has_side_effects=True, vmem_limit_bytes=60 * 1024 * 1024
        ),
    )(queries, keys, values, level_weights.transpose(1, 0, 2), out_weight)


def solution(mesh):
    in_specs = (
        P("seq", "head"),
        P("seq", "head"),
        P("seq", "head"),
        P("head", None, "seq"),
        P("head", None),
    )
    out_specs = P("seq", "head")
    return jax.shard_map(local, mesh=mesh, in_specs=in_specs, out_specs=out_specs, check_vma=False)
```

```python
import jax
import jax.numpy as jnp
from jax import lax
from jax.experimental import pallas as pl
from jax.experimental.pallas import tpu as pltpu
from jax.sharding import PartitionSpec as P

BLOCK = 128
EPS = 1e-06
LINE = 8
CHIPS = 4
PLANES = 8
FAR = 6
DIRECT = 256
NEAR = (1, 2, 3, PLANES - 3, PLANES - 2, PLANES - 1)
TAKERS = {0: (3, 2, 1), 1: (3, 2, 0), 2: (3, 0), 3: (0,), 4: (7, 6, 5), 5: (7, 6), 6: (7,)}
ROOTS = {3: (5, 4), 0: (6, 7)}
BF = jnp.bfloat16
F32 = jnp.float32
MESH = pl.DeviceIdType.MESH


def dot(a, b):
    return jnp.dot(a, b, preferred_element_type=F32)


def kernel(
    q_hbm,
    k_hbm,
    v_hbm,
    lw_hbm,
    w_hbm,
    out_ref,
    q_v,
    k_v,
    v_v,
    lw_v,
    lw_t,
    w_v,
    bst,
    stbuf,
    recv1,
    lowbuf,
    zrecv,
    states,
    qs,
    tot,
    nrm,
    p1s,
    p1r,
    p2s,
    p2r,
    mine,
    own,
    wp,
    pn,
    h2s,
    h2r,
    ownh,
    in_sem,
    p1_s,
    p1_r,
    core_s,
    core_r,
    z_s,
    z_r,
    low_s,
    low_r,
    mid_s,
    mid_r,
    hi_s,
    hi_r,
    y1_s,
    y1_r,
    y2_s,
    y2_r,
    wf_s,
    w_s,
    w_r,
    hy_s,
    hy_r,
    h2_s,
    h2_r,
):
    heads = stbuf.shape[0]
    tok = q_v.shape[0]
    nblk = tok // BLOCK
    p = lax.axis_index("seq")
    y = lax.axis_index("head")
    z = p // LINE
    d = p % LINE
    core = d % 2
    x = d // 2
    pa = y + 1 - 2 * (y % 2)
    pb = 3 - y
    opp = (y + 2) % 4

    def line(e):
        return (z * LINE + e, y)

    def local_in(i, src, dst):
        return pltpu.make_async_copy(src, dst, in_sem.at[i])

    cps = [
        local_in(0, k_hbm, k_v),
        local_in(1, v_hbm, v_v),
        local_in(2, q_hbm, q_v),
        local_in(3, lw_hbm, lw_v),
        local_in(4, w_hbm, w_v),
    ]
    cps[0].start()
    cps[1].start()

    barrier = pltpu.get_barrier_semaphore()
    for i in range(1, LINE):
        pl.semaphore_signal(barrier, inc=1, device_id=line((d + i) % LINE), device_id_type=MESH)
    for i in NEAR:
        pl.semaphore_signal(
            barrier, inc=1, device_id=(((z + i) % PLANES) * LINE + d, y), device_id_type=MESH
        )
    for t in (pa, pb):
        pl.semaphore_signal(barrier, inc=1, device_id=(p, t), device_id_type=MESH)

    def cols(h):
        return pl.ds(pl.multiple_of(h * 128, 128), 128)

    @pl.when(core == 0)
    def _():
        states[:, pl.ds(0, 128), :] = jnp.zeros((heads, 128, 128), BF)

    @pl.when(x % 2 == 0)
    def _():
        states[:, pl.ds(128, 128), :] = jnp.zeros((heads, 128, 128), BF)

    @pl.when(x < 2)
    def _():
        states[:, pl.ds(256, 128), :] = jnp.zeros((heads, 128, 128), BF)

    cps[0].wait()
    cps[1].wait()
    cps[2].start()
    cps[3].start()

    def key_head(h, _):
        kf = k_v[:, cols(h)].astype(F32)
        ku = (kf * lax.rsqrt(jnp.sum(kf * kf, axis=-1, keepdims=True) + EPS)).astype(BF)
        k_v[:, cols(h)] = ku
        vv = v_v[:, cols(h)]
        s = [
            lax.dot_general(
                ku[b * BLOCK : (b + 1) * BLOCK],
                vv[b * BLOCK : (b + 1) * BLOCK],
                (((0,), (0,)), ((), ())),
                preferred_element_type=F32,
            )
            for b in range(nblk)
        ]
        s01 = s[0] + s[1]
        bst[h, 0] = s[0].astype(BF)
        bst[h, 1] = s[2].astype(BF)
        bst[h, 2] = s01.astype(BF)
        stbuf[h] = (s01 + s[2] + s[3]).astype(BF)
        return 0

    lax.fori_loop(0, heads, key_head, 0, unroll=True)
    pl.semaphore_wait(barrier, LINE - 1 + len(NEAR) + 2)

    def send1(e):
        return pltpu.make_async_remote_copy(
            src_ref=stbuf.at[e],
            dst_ref=recv1.at[d],
            send_sem=p1_s.at[e],
            recv_sem=p1_r.at[d],
            device_id=line(e),
            device_id_type=MESH,
        )

    for i in (2, 1, 3):
        for c in range(2):
            send1(((x + i) % CHIPS) * 2 + c).start()
    send1(d + 1 - 2 * core).start()

    share = (w_hbm.shape[0] - DIRECT) // LINE
    width = out_ref.shape[1]

    def w_rows(h):
        return pl.ds(pl.multiple_of(DIRECT + h * share, 16), share)

    def chip_rows(c):
        return pl.ds(pl.multiple_of(c * (DIRECT // 2), 16), DIRECT // 2)

    def w_fetch(i):
        j = i % 2
        block = (pa, opp)[j]
        rows, piece = (w_rows(d), d) if i < 2 else (chip_rows(core), LINE + core)
        return pltpu.make_async_remote_copy(
            src_ref=w_hbm.at[rows, pl.ds(pl.multiple_of(block * width, width), width)],
            dst_ref=wp.at[j, rows, :],
            send_sem=wf_s.at[i],
            recv_sem=w_r.at[piece, j],
            device_id=(p, pa),
            device_id_type=MESH,
        )

    cps[4].start()
    fetches = 4 if DIRECT else 2
    for i in range(fetches):
        w_fetch(i).start()
    core_copy = pltpu.make_async_remote_copy(
        src_ref=stbuf,
        dst_ref=states.at[:, pl.ds(0, 128), :],
        send_sem=core_s,
        recv_sem=core_r,
        device_id=line(d + 1 - 2 * core),
        device_id_type=MESH,
    )

    @pl.when(core == 0)
    def _():
        core_copy.start()

    recv1[d] = stbuf[d]

    cps[2].wait()
    cps[3].wait()
    lw_all = lw_v[...].reshape(lw_v.shape[0] * heads, tok)
    lw_t[...] = jnp.concatenate([lw_all, jnp.zeros((128 - lw_all.shape[0], tok), F32)], axis=0).T

    def level_columns(h):
        return pltpu.roll(lw_t[...], lax.rem(128 - h, 128), 1)

    causal = lax.broadcasted_iota(jnp.int32, (BLOCK, BLOCK), 0) >= lax.broadcasted_iota(
        jnp.int32, (BLOCK, BLOCK), 1
    )

    def query_head(h, _):
        qf = q_v[:, cols(h)].astype(F32)
        qu = (qf * lax.rsqrt(jnp.sum(qf * qf, axis=-1, keepdims=True) + EPS)).astype(BF)
        q_v[:, cols(h)] = qu
        lwt = level_columns(h)
        for b in range(nblk):
            rows = pl.ds(b * BLOCK, BLOCK)
            part = slice(b * BLOCK, (b + 1) * BLOCK)
            qb = qu[part]
            s = lax.dot_general(
                qb, k_v[rows, cols(h)], (((1,), (1,)), ((), ())), preferred_element_type=F32
            )
            wgt = jnp.where(causal, s * lwt[part, 0:1], 0.0).astype(BF)
            acc = dot(wgt, v_v[rows, cols(h)])
            if b % 2 == 1:
                acc = acc + dot(qb, bst[h, b // 2]) * lwt[part, 8:9]
            if b >= 2:
                acc = acc + dot(qb, bst[h, 2]) * lwt[part, 16:17]
            tot[rows, cols(h)] = acc
        return 0

    lax.fori_loop(0, heads, query_head, 0, unroll=True)

    for i in range(1, LINE):
        e = (d + i) % LINE
        pltpu.make_async_remote_copy(
            src_ref=stbuf.at[e],
            dst_ref=recv1.at[e],
            send_sem=p1_s.at[e],
            recv_sem=p1_r.at[e],
            device_id=line(e),
            device_id_type=MESH,
        ).wait_recv()
    pair = [recv1[2 * c].astype(F32) + recv1[2 * c + 1].astype(F32) for c in range(CHIPS)]
    half = pair[0] + pair[1]
    zrecv[z] = (half + pair[2] + pair[3]).astype(BF)

    def zcopy(slot, src, t):
        return pltpu.make_async_remote_copy(
            src_ref=zrecv.at[src],
            dst_ref=zrecv.at[src],
            send_sem=z_s.at[slot],
            recv_sem=z_r.at[src],
            device_id=(t * LINE + d, y),
            device_id_type=MESH,
        )

    for src, takers in TAKERS.items():

        @pl.when(z == src)
        def _():
            for slot, t in enumerate(takers):
                zcopy(slot, src, t).start()

    none = jnp.zeros((128, 128), BF)
    for c in range(CHIPS):
        lowbuf[c, pl.ds(0, 128), :] = pair[c - 1].astype(BF) if c % 2 else none
        lowbuf[c, pl.ds(128, 128), :] = half.astype(BF) if c >= 2 else none

    mid_rows = pl.ds(384, 256)
    hi_rows = pl.ds(640, 128)

    def spread(src, rows, peer, s_sem, i, r_sem, h):
        return pltpu.make_async_remote_copy(
            src_ref=src,
            dst_ref=states.at[h, rows, :],
            send_sem=s_sem.at[i],
            recv_sem=r_sem.at[h],
            device_id=line(peer),
            device_id_type=MESH,
        )

    mate = d + 1 - 2 * core
    sends = []
    states[d, pl.ds(128, 256), :] = lowbuf[x]
    def low_copy(c, slot):
        first = 0 if c % 2 else 1
        count = 2 if c == 3 else 1
        return pltpu.make_async_remote_copy(
            src_ref=lowbuf.at[c, pl.ds(first * 128, count * 128), :],
            dst_ref=states.at[d, pl.ds(128 + first * 128, count * 128), :],
            send_sem=low_s.at[slot],
            recv_sem=low_r.at[d],
            device_id=line(mate if slot == 0 else c * 2 + core),
            device_id_type=MESH,
        )

    for c in range(1, CHIPS):

        @pl.when(x != c)
        def _():
            low_copy(c, c).start()

        @pl.when(x == c)
        def _():
            low_copy(c, 0).start()

    def scaled(h, levels):
        quf = q_v[:, cols(h)].astype(F32)
        lwt = level_columns(h)
        for lv in levels:
            col = 8 * (3 + lv)
            qs[h, :, lv * 128 : (lv + 1) * 128] = (quf * lwt[:, col : col + 1]).astype(BF)
        return 0

    def scale_low(h, _):
        return scaled(h, range(0, 3))

    def scale_high(h, _):
        return scaled(h, range(3, FAR))

    lax.fori_loop(0, heads, scale_low, 0, unroll=True)

    def low_forward(c):
        first = 0 if c % 2 else 1
        count = 2 if c == 3 else 1
        rows = pl.ds(128 + first * 128, count * 128)
        for i in range(1, CHIPS):
            h = ((c + i) % CHIPS) * 2 + core
            spread(states.at[h, rows, :], rows, mate, low_s, 0, low_r, h).wait_recv()
            spread(states.at[h, rows, :], rows, mate, low_s, CHIPS + i - 1, low_r, h).start()

    def low_landed(c):
        first = 0 if c % 2 else 1
        count = 2 if c == 3 else 1
        rows = pl.ds(128 + first * 128, count * 128)
        for i in range(CHIPS):
            h = i * 2 + 1 - core
            spread(states.at[h, rows, :], rows, mate, low_s, 0, low_r, h).wait_recv()

    def along_line(rows, s_sem, r_sem):
        src = states.at[d, rows, :]
        for i in (2, 1, 3, 0):
            e = ((x + i) % CHIPS) * 2 + core if i else mate
            cp = spread(src, rows, e, s_sem, i, r_sem, d)
            cp.start()
            sends.append(cp)

    def forward(rows, s_sem, r_sem):
        for i in (1, 3, 2):
            h = ((x + i) % CHIPS) * 2 + core
            src = states.at[h, rows, :]
            spread(src, rows, mate, s_sem, 0, r_sem, h).wait_recv()
            cp = spread(src, rows, mate, s_sem, 3 + i, r_sem, h)
            cp.start()
            sends.append(cp)

    def landed(rows, s_sem, r_sem):
        for i in range(CHIPS):
            h = i * 2 + 1 - core
            spread(states.at[h, rows, :], rows, mate, s_sem, 0, r_sem, h).wait_recv()

    for t in range(PLANES):

        @pl.when(z == t)
        def _():
            for src, takers in TAKERS.items():
                if t in takers:
                    zcopy(0, src, t).wait_recv()

    def put(row, val):
        states[d, pl.ds(row, 128), :] = val

    for root, takers in ROOTS.items():

        @pl.when(z == root)
        def _():
            q4 = [zrecv[i].astype(F32) for i in range(4)]
            zrecv[PLANES] = (q4[0] + q4[1] + q4[2] + q4[3]).astype(BF)
            for slot, t in enumerate(takers):
                zcopy(3 + slot, PLANES, t).start()

    base = (z // 4) * 4

    @pl.when(z % 2 == 1)
    def _():
        put(384, zrecv[z - 1])

    @pl.when(z % 2 == 0)
    def _():
        put(384, none)

    @pl.when((z // 2) % 2 == 1)
    def _():
        put(512, (zrecv[base].astype(F32) + zrecv[base + 1].astype(F32)).astype(BF))

    @pl.when((z // 2) % 2 == 0)
    def _():
        put(512, none)

    along_line(mid_rows, mid_s, mid_r)
    lax.fori_loop(0, heads, scale_high, 0, unroll=True)
    for c in range(1, CHIPS):

        @pl.when(x == c)
        def _():
            low_forward(c)

    @pl.when(z >= 4)
    def _():
        zcopy(0, PLANES, 0).wait_recv()
        put(640, zrecv[PLANES])

    @pl.when(z < 4)
    def _():
        put(640, none)

    along_line(hi_rows, hi_s, hi_r)
    for c in range(1, CHIPS):

        @pl.when(x == c)
        def _():
            low_landed(c)

    @pl.when(core == 1)
    def _():
        core_copy.wait_recv()

    def low_head(h, _):
        tot[:, cols(h)] += dot(qs[h, :, 0:384], states[h, 0:384, :])
        return 0

    lax.fori_loop(0, heads, low_head, 0, unroll=True)

    forward(mid_rows, mid_s, mid_r)
    ahead = (x + 1 + 2 * core) % CHIPS
    behind = (x + 3 - 2 * core) % CHIPS

    def w_move(h, j, peer, slot, rows=None):
        rows = w_rows(h) if rows is None else rows
        return pltpu.make_async_remote_copy(
            src_ref=wp.at[j, rows, :],
            dst_ref=wp.at[j, rows, :],
            send_sem=w_s.at[slot, j],
            recv_sem=w_r.at[h, j],
            device_id=line(peer),
            device_id_type=MESH,
        )

    def w_send(h, j, peer, slot):
        cp = w_move(h, j, peer, slot)
        cp.start()
        sends.append(cp)

    for j in range(2):
        w_move(d, j, mate, 0).wait_recv()
        w_send(d, j, ahead * 2 + core, 0)
        w_send(d, j, behind * 2 + core, 1)
        w_send(d, j, mate, 2)

    landed(mid_rows, mid_s, mid_r)

    def mid_head(h, _):
        tot[:, cols(h)] += dot(qs[h, :, 384:640], states[h, 384:640, :])
        return 0

    forward(hi_rows, hi_s, hi_r)
    lax.fori_loop(0, heads, mid_head, 0, unroll=True)

    landed(hi_rows, hi_s, hi_r)

    top = p1s.shape[2]
    lead = 2 * top

    def normalize(lo, n):
        rows = pl.ds(lo, n)

        def norm_head(h, _):
            a = tot[rows, cols(h)] + dot(qs[h, rows, 640:768], states[h, 640:768, :])
            m = jnp.mean(a * a, axis=-1, keepdims=True)
            nrm[rows, cols(h)] = (a * lax.rsqrt(m + EPS)).astype(BF)
            return 0

        lax.fori_loop(0, heads, norm_head, 0, unroll=True)

    normalize(0, lead)
    cps[4].wait()

    tiles = mine.shape[1]
    tw = width // tiles

    def w_tile(block, t):
        return w_v[:, pl.ds(pl.multiple_of(block * width + t * tw, tw), tw)]

    def tile_product(block, t):
        return dot(nrm[pl.ds(0, lead), :], w_tile(block, t))

    def y1(side, i):
        return pltpu.make_async_remote_copy(
            src_ref=p1s.at[side, i],
            dst_ref=p1r.at[side, i],
            send_sem=y1_s.at[side, i],
            recv_sem=y1_r.at[side, i],
            device_id=(p, (pa, pb)[side]),
            device_id_type=MESH,
        )

    def y2(side, i):
        return pltpu.make_async_remote_copy(
            src_ref=p2s.at[side, i],
            dst_ref=p2r.at[side, i],
            send_sem=y2_s.at[side, i],
            recv_sem=y2_r.at[side, i],
            device_id=(p, (pa, pb)[side]),
            device_id_type=MESH,
        )

    def far_tile(t, _):
        prod = tile_product(opp, t)
        p1s[0, t] = prod[:top].astype(BF)
        y1(0, t).start()
        p1s[1, t] = prod[top:].astype(BF)
        y1(1, t).start()
        return 0

    lax.fori_loop(0, tiles, far_tile, 0)
    part = pn.shape[1]
    parts = pn.shape[0]

    def normed_copy(c):
        return pltpu.make_async_remote_copy(
            src_ref=nrm.at[pl.ds(lead + c * part, part), :],
            dst_ref=pn.at[c],
            send_sem=hy_s.at[c],
            recv_sem=hy_r.at[c],
            device_id=(p, pa),
            device_id_type=MESH,
        )

    for c in range(parts):
        normalize(lead + c * part, part)
        normed_copy(c).start()

    def side_tile(t, _):
        prod = tile_product(pa, t)
        p1s[0, tiles + t] = prod[:top].astype(BF)
        y1(0, tiles + t).start()
        mine[0, t] = prod[top:]
        prod = tile_product(pb, t)
        p1s[1, tiles + t] = prod[top:].astype(BF)
        y1(1, tiles + t).start()
        mine[1, t] = prod[:top]
        return 0

    lax.fori_loop(0, tiles, side_tile, 0)

    def second(t, _):
        y1(1, t).wait_recv()
        p2s[0, t] = (mine[0, t] + p1r[1, t].astype(F32)).astype(BF)
        y2(0, t).start()
        y1(0, t).wait_recv()
        p2s[1, t] = (mine[1, t] + p1r[0, t].astype(F32)).astype(BF)
        y2(1, t).start()
        return 0

    def own_tile(t, _):
        own[t] = tile_product(y, t)
        return 0

    if DIRECT:
        for j in range(2):
            w_move(LINE + core, j, mate, 7, chip_rows(core)).wait_recv()
            cp = w_move(LINE + core, j, mate, 7, chip_rows(core))
            cp.start()
            sends.append(cp)
    for j in range(2):
        h = behind * 2 + core
        w_move(h, j, mate, 0).wait_recv()
        w_send(h, j, ahead * 2 + core, 3)
        w_send(h, j, mate, 4)
    for j in range(2):
        h = ahead * 2 + core
        w_move(h, j, mate, 0).wait_recv()
        w_send(h, j, mate, 5)
    lax.fori_loop(0, tiles, own_tile, 0)
    lax.fori_loop(0, tiles, second, 0)
    for j in range(2):
        h = ((x + 2) % CHIPS) * 2 + core
        w_move(h, j, mate, 0).wait_recv()
        w_send(h, j, mate, 6)
    for j in range(2):
        for i in range(CHIPS):
            w_move(i * 2 + 1 - core, j, mate, 0).wait_recv()
        if DIRECT:
            w_move(LINE + 1 - core, j, mate, 0, chip_rows(1 - core)).wait_recv()

    def h2(c, t):
        return pltpu.make_async_remote_copy(
            src_ref=h2s.at[c, t],
            dst_ref=h2r.at[c, t],
            send_sem=h2_s.at[c, t],
            recv_sem=h2_r.at[c, t],
            device_id=(p, pb),
            device_id_type=MESH,
        )

    def both(c, block, j, t):
        lanes = pl.ds(pl.multiple_of(t * tw, tw), tw)
        own_rows = nrm[pl.ds(lead + c * part, part), :]
        return dot(own_rows, w_tile(block, t)) + dot(pn[c], wp[j, :, lanes])

    for c in range(parts):
        normed_copy(c).wait_recv()

        def give_tile(t, _):
            h2s[c, t] = both(c, pb, 1, t).astype(BF)
            h2(c, t).start()
            return 0

        lax.fori_loop(0, tiles, give_tile, 0)

    for c in range(parts):

        def keep_tile(t, _):
            ownh[c, t] = both(c, y, 0, t)
            return 0

        lax.fori_loop(0, tiles, keep_tile, 0)

    def last(t, _):
        lanes = pl.ds(pl.multiple_of(t * tw, tw), tw)
        y1(0, tiles + t).wait_recv()
        y2(1, t).wait_recv()
        out_ref[pl.ds(0, top), lanes] = (
            own[t, pl.ds(0, top), :] + p1r[0, tiles + t].astype(F32) + p2r[1, t].astype(F32)
        ).astype(BF)
        y1(1, tiles + t).wait_recv()
        y2(0, t).wait_recv()
        out_ref[pl.ds(top, top), lanes] = (
            own[t, pl.ds(top, top), :] + p1r[1, tiles + t].astype(F32) + p2r[0, t].astype(F32)
        ).astype(BF)
        return 0

    lax.fori_loop(0, tiles, last, 0)
    for c in range(parts):

        def last_given(t, _):
            lanes = pl.ds(pl.multiple_of(t * tw, tw), tw)
            h2(c, t).wait_recv()
            out_ref[pl.ds(lead + c * part, part), lanes] = (
                ownh[c, t] + h2r[c, t].astype(F32)
            ).astype(BF)
            return 0

        lax.fori_loop(0, tiles, last_given, 0)

    for i in range(fetches):
        w_fetch(i).wait_send()
    for c in range(parts):
        normed_copy(c).wait_send()

        def drain3(t, _):
            h2(c, t).wait_send()
            return 0

        lax.fori_loop(0, tiles, drain3, 0)

    for i in range(1, LINE):
        send1((d + i) % LINE).wait_send()

    @pl.when(core == 0)
    def _():
        core_copy.wait_send()

    for src in range(PLANES):

        @pl.when(z == src)
        def _():
            for slot, t in enumerate(TAKERS.get(src, ())):
                zcopy(slot, src, t).wait_send()
            for slot, t in enumerate(ROOTS.get(src, ())):
                zcopy(3 + slot, PLANES, t).wait_send()

    for c in range(1, CHIPS):

        @pl.when(x != c)
        def _():
            low_copy(c, c).wait_send()

        @pl.when(x == c)
        def _():
            low_copy(c, 0).wait_send()
            first = 0 if c % 2 else 1
            count = 2 if c == 3 else 1
            rows = pl.ds(128 + first * 128, count * 128)
            for i in range(1, CHIPS):
                spread(
                    states.at[0, rows, :], rows, mate, low_s, CHIPS + i - 1, low_r, 0
                ).wait_send()

    for cp in sends:
        cp.wait_send()
    for side in range(2):

        def drain(i, _):
            y1(side, i).wait_send()
            return 0

        lax.fori_loop(0, 2 * tiles, drain, 0)

        def drain2(i, _):
            y2(side, i).wait_send()
            return 0

        lax.fori_loop(0, tiles, drain2, 0)


def local(queries, keys, values, level_weights, out_weight):
    tok, width = queries.shape
    heads, levels, _ = level_weights.shape
    tiles = 4
    top = 96
    parts = 2
    part = (tok - 2 * top) // parts
    tw = width // tiles
    dma = pltpu.SemaphoreType.DMA
    scratch = [
        pltpu.VMEM((tok, width), BF),
        pltpu.VMEM((tok, width), BF),
        pltpu.VMEM((tok, width), BF),
        pltpu.VMEM((levels, heads, tok), F32),
        pltpu.VMEM((tok, 128), F32),
        pltpu.VMEM(out_weight.shape, BF),
        pltpu.VMEM((heads, 3, 128, 128), BF),
        pltpu.VMEM((heads, 128, 128), BF),
        pltpu.VMEM((LINE, 128, 128), BF),
        pltpu.VMEM((CHIPS, 256, 128), BF),
        pltpu.VMEM((PLANES + 1, 128, 128), BF),
        pltpu.VMEM((heads, FAR * 128, 128), BF),
        pltpu.VMEM((heads, tok, FAR * 128), BF),
        pltpu.VMEM((tok, width), F32),
        pltpu.VMEM((tok, width), BF),
        pltpu.VMEM((2, 2 * tiles, top, tw), BF),
        pltpu.VMEM((2, 2 * tiles, top, tw), BF),
        pltpu.VMEM((2, tiles, top, tw), BF),
        pltpu.VMEM((2, tiles, top, tw), BF),
        pltpu.VMEM((2, tiles, top, tw), F32),
        pltpu.VMEM((tiles, 2 * top, tw), F32),
        pltpu.VMEM((2, width, width), BF),
        pltpu.VMEM((parts, part, width), BF),
        pltpu.VMEM((parts, tiles, part, tw), BF),
        pltpu.VMEM((parts, tiles, part, tw), BF),
        pltpu.VMEM((parts, tiles, part, tw), F32),
        dma((5,)),
        dma((LINE,)),
        dma((LINE,)),
        dma,
        dma,
        dma((5,)),
        dma((PLANES + 1,)),
        dma((2 * CHIPS,)),
        dma((LINE,)),
        dma((2 * CHIPS,)),
        dma((LINE,)),
        dma((2 * CHIPS,)),
        dma((LINE,)),
        dma((2, 2 * tiles)),
        dma((2, 2 * tiles)),
        dma((2, tiles)),
        dma((2, tiles)),
        dma((4,)),
        dma((8, 2)),
        dma((LINE + 2, 2)),
        dma((parts,)),
        dma((parts,)),
        dma((parts, tiles)),
        dma((parts, tiles)),
    ]
    return pl.pallas_call(
        kernel,
        out_shape=pltpu.VMEM((tok, width), BF),
        in_specs=[pl.BlockSpec(memory_space=pl.ANY)] * 5,
        out_specs=pl.BlockSpec(memory_space=pltpu.VMEM),
        scratch_shapes=scratch,
        compiler_params=pltpu.CompilerParams(
            collective_id=0, has_side_effects=True, vmem_limit_bytes=60 * 1024 * 1024
        ),
    )(queries, keys, values, level_weights.transpose(1, 0, 2), out_weight)


def solution(mesh):
    in_specs = (
        P("seq", "head"),
        P("seq", "head"),
        P("seq", "head"),
        P("head", None, "seq"),
        P("head", None),
    )
    out_specs = P("seq", "head")
    return jax.shard_map(local, mesh=mesh, in_specs=in_specs, out_specs=out_specs, check_vma=False)
```

```python
import jax
import jax.numpy as jnp
from jax import lax
from jax.experimental import pallas as pl
from jax.experimental.pallas import tpu as pltpu
from jax.sharding import PartitionSpec as P

BLOCK = 128
EPS = 1e-06
LINE = 8
CHIPS = 4
PLANES = 8
FAR = 6
DIRECT = 256
NEAR = (1, 2, 3, PLANES - 3, PLANES - 2, PLANES - 1)
TAKERS = {0: (3, 2, 1), 1: (3, 2, 0), 2: (3, 0), 3: (0,), 4: (7, 6, 5), 5: (7, 6), 6: (7,)}
ROOTS = {3: (5, 4), 0: (6, 7)}
BF = jnp.bfloat16
F32 = jnp.float32
MESH = pl.DeviceIdType.MESH


def dot(a, b):
    return jnp.dot(a, b, preferred_element_type=F32)


def kernel(
    q_hbm,
    k_hbm,
    v_hbm,
    lw_hbm,
    w_hbm,
    out_ref,
    q_v,
    k_v,
    v_v,
    lw_v,
    lw_t,
    w_v,
    bst,
    stbuf,
    recv1,
    lowbuf,
    zrecv,
    states,
    qs,
    tot,
    nrm,
    p1s,
    p1r,
    p2s,
    p2r,
    mine,
    own,
    wp,
    pn,
    h2s,
    h2r,
    ownh,
    in_sem,
    p1_s,
    p1_r,
    core_s,
    core_r,
    z_s,
    z_r,
    low_s,
    low_r,
    mid_s,
    mid_r,
    hi_s,
    hi_r,
    y1_s,
    y1_r,
    y2_s,
    y2_r,
    wf_s,
    w_s,
    w_r,
    hy_s,
    hy_r,
    h2_s,
    h2_r,
):
    heads = stbuf.shape[0]
    tok = q_v.shape[0]
    nblk = tok // BLOCK
    p = lax.axis_index("seq")
    y = lax.axis_index("head")
    z = p // LINE
    d = p % LINE
    core = d % 2
    x = d // 2
    pa = y + 1 - 2 * (y % 2)
    pb = 3 - y
    opp = (y + 2) % 4

    def line(e):
        return (z * LINE + e, y)

    def local_in(i, src, dst):
        return pltpu.make_async_copy(src, dst, in_sem.at[i])

    cps = [
        local_in(0, k_hbm, k_v),
        local_in(1, v_hbm, v_v),
        local_in(2, q_hbm, q_v),
        local_in(3, lw_hbm, lw_v),
        local_in(4, w_hbm, w_v),
    ]
    cps[0].start()
    cps[1].start()

    barrier = pltpu.get_barrier_semaphore()
    for i in range(1, LINE):
        pl.semaphore_signal(barrier, inc=1, device_id=line((d + i) % LINE), device_id_type=MESH)
    for i in NEAR:
        pl.semaphore_signal(
            barrier, inc=1, device_id=(((z + i) % PLANES) * LINE + d, y), device_id_type=MESH
        )
    for t in (pa, pb):
        pl.semaphore_signal(barrier, inc=1, device_id=(p, t), device_id_type=MESH)

    def cols(h):
        return pl.ds(pl.multiple_of(h * 128, 128), 128)

    @pl.when(core == 0)
    def _():
        states[:, pl.ds(0, 128), :] = jnp.zeros((heads, 128, 128), BF)

    @pl.when(x % 2 == 0)
    def _():
        states[:, pl.ds(128, 128), :] = jnp.zeros((heads, 128, 128), BF)

    @pl.when(x < 2)
    def _():
        states[:, pl.ds(256, 128), :] = jnp.zeros((heads, 128, 128), BF)

    cps[0].wait()
    cps[1].wait()
    cps[2].start()
    cps[3].start()

    def key_head(h, _):
        kf = k_v[:, cols(h)].astype(F32)
        ku = (kf * lax.rsqrt(jnp.sum(kf * kf, axis=-1, keepdims=True) + EPS)).astype(BF)
        k_v[:, cols(h)] = ku
        vv = v_v[:, cols(h)]
        s = [
            lax.dot_general(
                ku[b * BLOCK : (b + 1) * BLOCK],
                vv[b * BLOCK : (b + 1) * BLOCK],
                (((0,), (0,)), ((), ())),
                preferred_element_type=F32,
            )
            for b in range(nblk)
        ]
        s01 = s[0] + s[1]
        bst[h, 0] = s[0].astype(BF)
        bst[h, 1] = s[2].astype(BF)
        bst[h, 2] = s01.astype(BF)
        stbuf[h] = (s01 + s[2] + s[3]).astype(BF)
        return 0

    lax.fori_loop(0, heads, key_head, 0, unroll=True)
    pl.semaphore_wait(barrier, LINE - 1 + len(NEAR) + 2)

    def send1(e):
        return pltpu.make_async_remote_copy(
            src_ref=stbuf.at[e],
            dst_ref=recv1.at[d],
            send_sem=p1_s.at[e],
            recv_sem=p1_r.at[d],
            device_id=line(e),
            device_id_type=MESH,
        )

    for i in (2, 1, 3):
        for c in range(2):
            send1(((x + i) % CHIPS) * 2 + c).start()
    send1(d + 1 - 2 * core).start()

    share = (w_hbm.shape[0] - DIRECT) // LINE
    width = out_ref.shape[1]

    def w_rows(h):
        return pl.ds(pl.multiple_of(DIRECT + h * share, 16), share)

    def chip_rows(c):
        return pl.ds(pl.multiple_of(c * (DIRECT // 2), 16), DIRECT // 2)

    def w_fetch(i):
        j = i % 2
        block = (pa, opp)[j]
        rows, piece = (w_rows(d), d) if i < 2 else (chip_rows(core), LINE + core)
        return pltpu.make_async_remote_copy(
            src_ref=w_hbm.at[rows, pl.ds(pl.multiple_of(block * width, width), width)],
            dst_ref=wp.at[j, rows, :],
            send_sem=wf_s.at[i],
            recv_sem=w_r.at[piece, j],
            device_id=(p, pa),
            device_id_type=MESH,
        )

    cps[4].start()
    fetches = 4 if DIRECT else 2
    for i in range(fetches):
        w_fetch(i).start()
    core_copy = pltpu.make_async_remote_copy(
        src_ref=stbuf,
        dst_ref=states.at[:, pl.ds(0, 128), :],
        send_sem=core_s,
        recv_sem=core_r,
        device_id=line(d + 1 - 2 * core),
        device_id_type=MESH,
    )

    @pl.when(core == 0)
    def _():
        core_copy.start()

    recv1[d] = stbuf[d]

    cps[2].wait()
    cps[3].wait()
    lw_all = lw_v[...].reshape(lw_v.shape[0] * heads, tok)
    lw_t[...] = jnp.concatenate([lw_all, jnp.zeros((128 - lw_all.shape[0], tok), F32)], axis=0).T

    def level_columns(h):
        return pltpu.roll(lw_t[...], lax.rem(128 - h, 128), 1)

    causal = lax.broadcasted_iota(jnp.int32, (BLOCK, BLOCK), 0) >= lax.broadcasted_iota(
        jnp.int32, (BLOCK, BLOCK), 1
    )

    def query_head(h, _):
        qf = q_v[:, cols(h)].astype(F32)
        qu = (qf * lax.rsqrt(jnp.sum(qf * qf, axis=-1, keepdims=True) + EPS)).astype(BF)
        q_v[:, cols(h)] = qu
        lwt = level_columns(h)
        for b in range(nblk):
            rows = pl.ds(b * BLOCK, BLOCK)
            part = slice(b * BLOCK, (b + 1) * BLOCK)
            qb = qu[part]
            s = lax.dot_general(
                qb, k_v[rows, cols(h)], (((1,), (1,)), ((), ())), preferred_element_type=F32
            )
            wgt = jnp.where(causal, s * lwt[part, 0:1], 0.0).astype(BF)
            acc = dot(wgt, v_v[rows, cols(h)])
            if b % 2 == 1:
                acc = acc + dot(qb, bst[h, b // 2]) * lwt[part, 8:9]
            if b >= 2:
                acc = acc + dot(qb, bst[h, 2]) * lwt[part, 16:17]
            tot[rows, cols(h)] = acc
        return 0

    lax.fori_loop(0, heads, query_head, 0, unroll=True)

    for i in range(1, LINE):
        e = (d + i) % LINE
        pltpu.make_async_remote_copy(
            src_ref=stbuf.at[e],
            dst_ref=recv1.at[e],
            send_sem=p1_s.at[e],
            recv_sem=p1_r.at[e],
            device_id=line(e),
            device_id_type=MESH,
        ).wait_recv()
    pair = [recv1[2 * c].astype(F32) + recv1[2 * c + 1].astype(F32) for c in range(CHIPS)]
    half = pair[0] + pair[1]
    zrecv[z] = (half + pair[2] + pair[3]).astype(BF)

    def zcopy(slot, src, t):
        return pltpu.make_async_remote_copy(
            src_ref=zrecv.at[src],
            dst_ref=zrecv.at[src],
            send_sem=z_s.at[slot],
            recv_sem=z_r.at[src],
            device_id=(t * LINE + d, y),
            device_id_type=MESH,
        )

    for src, takers in TAKERS.items():

        @pl.when(z == src)
        def _():
            for slot, t in enumerate(takers):
                zcopy(slot, src, t).start()

    none = jnp.zeros((128, 128), BF)
    for c in range(CHIPS):
        lowbuf[c, pl.ds(0, 128), :] = pair[c - 1].astype(BF) if c % 2 else none
        lowbuf[c, pl.ds(128, 128), :] = half.astype(BF) if c >= 2 else none

    mid_rows = pl.ds(384, 256)
    hi_rows = pl.ds(640, 128)

    def spread(src, rows, peer, s_sem, i, r_sem, h):
        return pltpu.make_async_remote_copy(
            src_ref=src,
            dst_ref=states.at[h, rows, :],
            send_sem=s_sem.at[i],
            recv_sem=r_sem.at[h],
            device_id=line(peer),
            device_id_type=MESH,
        )

    mate = d + 1 - 2 * core
    sends = []
    states[d, pl.ds(128, 256), :] = lowbuf[x]
    def low_copy(c, slot):
        first = 0 if c % 2 else 1
        count = 2 if c == 3 else 1
        return pltpu.make_async_remote_copy(
            src_ref=lowbuf.at[c, pl.ds(first * 128, count * 128), :],
            dst_ref=states.at[d, pl.ds(128 + first * 128, count * 128), :],
            send_sem=low_s.at[slot],
            recv_sem=low_r.at[d],
            device_id=line(mate if slot == 0 else c * 2 + core),
            device_id_type=MESH,
        )

    for c in range(1, CHIPS):

        @pl.when(x != c)
        def _():
            low_copy(c, c).start()

        @pl.when(x == c)
        def _():
            low_copy(c, 0).start()

    def scaled(h, levels):
        quf = q_v[:, cols(h)].astype(F32)
        lwt = level_columns(h)
        for lv in levels:
            col = 8 * (3 + lv)
            qs[h, :, lv * 128 : (lv + 1) * 128] = (quf * lwt[:, col : col + 1]).astype(BF)
        return 0

    def scale_low(h, _):
        return scaled(h, range(0, 3))

    def scale_high(h, _):
        return scaled(h, range(3, FAR))

    lax.fori_loop(0, heads, scale_low, 0, unroll=True)

    def low_forward(c):
        first = 0 if c % 2 else 1
        count = 2 if c == 3 else 1
        rows = pl.ds(128 + first * 128, count * 128)
        for i in range(1, CHIPS):
            h = ((c + i) % CHIPS) * 2 + core
            spread(states.at[h, rows, :], rows, mate, low_s, 0, low_r, h).wait_recv()
            spread(states.at[h, rows, :], rows, mate, low_s, CHIPS + i - 1, low_r, h).start()

    def low_landed(c):
        first = 0 if c % 2 else 1
        count = 2 if c == 3 else 1
        rows = pl.ds(128 + first * 128, count * 128)
        for i in range(CHIPS):
            h = i * 2 + 1 - core
            spread(states.at[h, rows, :], rows, mate, low_s, 0, low_r, h).wait_recv()

    def along_line(rows, s_sem, r_sem):
        src = states.at[d, rows, :]
        for i in (2, 1, 3, 0):
            e = ((x + i) % CHIPS) * 2 + core if i else mate
            cp = spread(src, rows, e, s_sem, i, r_sem, d)
            cp.start()
            sends.append(cp)

    def forward(rows, s_sem, r_sem):
        for i in (1, 3, 2):
            h = ((x + i) % CHIPS) * 2 + core
            src = states.at[h, rows, :]
            spread(src, rows, mate, s_sem, 0, r_sem, h).wait_recv()
            cp = spread(src, rows, mate, s_sem, 3 + i, r_sem, h)
            cp.start()
            sends.append(cp)

    def landed(rows, s_sem, r_sem):
        for i in range(CHIPS):
            h = i * 2 + 1 - core
            spread(states.at[h, rows, :], rows, mate, s_sem, 0, r_sem, h).wait_recv()

    for t in range(PLANES):

        @pl.when(z == t)
        def _():
            for src, takers in TAKERS.items():
                if t in takers:
                    zcopy(0, src, t).wait_recv()

    def put(row, val):
        states[d, pl.ds(row, 128), :] = val

    for root, takers in ROOTS.items():

        @pl.when(z == root)
        def _():
            q4 = [zrecv[i].astype(F32) for i in range(4)]
            zrecv[PLANES] = (q4[0] + q4[1] + q4[2] + q4[3]).astype(BF)
            for slot, t in enumerate(takers):
                zcopy(3 + slot, PLANES, t).start()

    base = (z // 4) * 4

    @pl.when(z % 2 == 1)
    def _():
        put(384, zrecv[z - 1])

    @pl.when(z % 2 == 0)
    def _():
        put(384, none)

    @pl.when((z // 2) % 2 == 1)
    def _():
        put(512, (zrecv[base].astype(F32) + zrecv[base + 1].astype(F32)).astype(BF))

    @pl.when((z // 2) % 2 == 0)
    def _():
        put(512, none)

    along_line(mid_rows, mid_s, mid_r)
    lax.fori_loop(0, heads, scale_high, 0, unroll=True)
    for c in range(1, CHIPS):

        @pl.when(x == c)
        def _():
            low_forward(c)

    @pl.when(z >= 4)
    def _():
        zcopy(0, PLANES, 0).wait_recv()
        put(640, zrecv[PLANES])

    @pl.when(z < 4)
    def _():
        put(640, none)

    along_line(hi_rows, hi_s, hi_r)
    for c in range(1, CHIPS):

        @pl.when(x == c)
        def _():
            low_landed(c)

    @pl.when(core == 1)
    def _():
        core_copy.wait_recv()

    def low_head(h, _):
        tot[:, cols(h)] += dot(qs[h, :, 0:384], states[h, 0:384, :])
        return 0

    lax.fori_loop(0, heads, low_head, 0, unroll=True)

    forward(mid_rows, mid_s, mid_r)
    ahead = (x + 1 + 2 * core) % CHIPS
    behind = (x + 3 - 2 * core) % CHIPS

    def w_move(h, j, peer, slot, rows=None):
        rows = w_rows(h) if rows is None else rows
        return pltpu.make_async_remote_copy(
            src_ref=wp.at[j, rows, :],
            dst_ref=wp.at[j, rows, :],
            send_sem=w_s.at[slot, j],
            recv_sem=w_r.at[h, j],
            device_id=line(peer),
            device_id_type=MESH,
        )

    def w_send(h, j, peer, slot):
        cp = w_move(h, j, peer, slot)
        cp.start()
        sends.append(cp)

    for j in range(2):
        w_move(d, j, mate, 0).wait_recv()
        w_send(d, j, ahead * 2 + core, 0)
        w_send(d, j, behind * 2 + core, 1)
        w_send(d, j, mate, 2)

    landed(mid_rows, mid_s, mid_r)

    def mid_head(h, _):
        tot[:, cols(h)] += dot(qs[h, :, 384:640], states[h, 384:640, :])
        return 0

    forward(hi_rows, hi_s, hi_r)
    lax.fori_loop(0, heads, mid_head, 0, unroll=True)

    landed(hi_rows, hi_s, hi_r)

    top = p1s.shape[2]
    lead = 2 * top

    def normalize(lo, n):
        rows = pl.ds(lo, n)

        def norm_head(h, _):
            a = tot[rows, cols(h)] + dot(qs[h, rows, 640:768], states[h, 640:768, :])
            m = jnp.mean(a * a, axis=-1, keepdims=True)
            nrm[rows, cols(h)] = (a * lax.rsqrt(m + EPS)).astype(BF)
            return 0

        lax.fori_loop(0, heads, norm_head, 0, unroll=True)

    normalize(0, lead)
    cps[4].wait()

    tiles = mine.shape[1]
    tw = width // tiles

    def w_tile(block, t):
        return w_v[:, pl.ds(pl.multiple_of(block * width + t * tw, tw), tw)]

    def tile_product(block, t):
        return dot(nrm[pl.ds(0, lead), :], w_tile(block, t))

    def y1(side, i):
        return pltpu.make_async_remote_copy(
            src_ref=p1s.at[side, i],
            dst_ref=p1r.at[side, i],
            send_sem=y1_s.at[side, i],
            recv_sem=y1_r.at[side, i],
            device_id=(p, (pa, pb)[side]),
            device_id_type=MESH,
        )

    def y2(side, i):
        return pltpu.make_async_remote_copy(
            src_ref=p2s.at[side, i],
            dst_ref=p2r.at[side, i],
            send_sem=y2_s.at[side, i],
            recv_sem=y2_r.at[side, i],
            device_id=(p, (pa, pb)[side]),
            device_id_type=MESH,
        )

    def far_tile(t, _):
        prod = tile_product(opp, t)
        p1s[0, t] = prod[:top].astype(BF)
        y1(0, t).start()
        p1s[1, t] = prod[top:].astype(BF)
        y1(1, t).start()
        return 0

    lax.fori_loop(0, tiles, far_tile, 0)
    part = pn.shape[1]
    parts = pn.shape[0]

    def normed_copy(c):
        return pltpu.make_async_remote_copy(
            src_ref=nrm.at[pl.ds(lead + c * part, part), :],
            dst_ref=pn.at[c],
            send_sem=hy_s.at[c],
            recv_sem=hy_r.at[c],
            device_id=(p, pa),
            device_id_type=MESH,
        )

    for c in range(parts):
        normalize(lead + c * part, part)
        normed_copy(c).start()

    def side_tile(t, _):
        prod = tile_product(pa, t)
        p1s[0, tiles + t] = prod[:top].astype(BF)
        y1(0, tiles + t).start()
        mine[0, t] = prod[top:]
        prod = tile_product(pb, t)
        p1s[1, tiles + t] = prod[top:].astype(BF)
        y1(1, tiles + t).start()
        mine[1, t] = prod[:top]
        return 0

    lax.fori_loop(0, tiles, side_tile, 0)

    def second(t, _):
        y1(1, t).wait_recv()
        p2s[0, t] = (mine[0, t] + p1r[1, t].astype(F32)).astype(BF)
        y2(0, t).start()
        y1(0, t).wait_recv()
        p2s[1, t] = (mine[1, t] + p1r[0, t].astype(F32)).astype(BF)
        y2(1, t).start()
        return 0

    def own_tile(t, _):
        own[t] = tile_product(y, t)
        return 0

    for j in range(2):
        h = behind * 2 + core
        w_move(h, j, mate, 0).wait_recv()
        w_send(h, j, ahead * 2 + core, 3)
        w_send(h, j, mate, 4)
    for j in range(2):
        h = ahead * 2 + core
        w_move(h, j, mate, 0).wait_recv()
        w_send(h, j, mate, 5)
    if DIRECT:
        for j in range(2):
            w_move(LINE + core, j, mate, 7, chip_rows(core)).wait_recv()
            cp = w_move(LINE + core, j, mate, 7, chip_rows(core))
            cp.start()
            sends.append(cp)
    lax.fori_loop(0, tiles, second, 0)
    lax.fori_loop(0, tiles, own_tile, 0)
    for j in range(2):
        h = ((x + 2) % CHIPS) * 2 + core
        w_move(h, j, mate, 0).wait_recv()
        w_send(h, j, mate, 6)
    for j in range(2):
        for i in range(CHIPS):
            w_move(i * 2 + 1 - core, j, mate, 0).wait_recv()
        if DIRECT:
            w_move(LINE + 1 - core, j, mate, 0, chip_rows(1 - core)).wait_recv()

    def h2(c, t):
        return pltpu.make_async_remote_copy(
            src_ref=h2s.at[c, t],
            dst_ref=h2r.at[c, t],
            send_sem=h2_s.at[c, t],
            recv_sem=h2_r.at[c, t],
            device_id=(p, pb),
            device_id_type=MESH,
        )

    def both(c, block, j, t):
        lanes = pl.ds(pl.multiple_of(t * tw, tw), tw)
        own_rows = nrm[pl.ds(lead + c * part, part), :]
        return dot(own_rows, w_tile(block, t)) + dot(pn[c], wp[j, :, lanes])

    for c in range(parts):
        normed_copy(c).wait_recv()

        def give_tile(t, _):
            h2s[c, t] = both(c, pb, 1, t).astype(BF)
            h2(c, t).start()
            return 0

        lax.fori_loop(0, tiles, give_tile, 0)

    for c in range(parts):

        def keep_tile(t, _):
            ownh[c, t] = both(c, y, 0, t)
            return 0

        lax.fori_loop(0, tiles, keep_tile, 0)

    def last(t, _):
        lanes = pl.ds(pl.multiple_of(t * tw, tw), tw)
        y1(0, tiles + t).wait_recv()
        y2(1, t).wait_recv()
        out_ref[pl.ds(0, top), lanes] = (
            own[t, pl.ds(0, top), :] + p1r[0, tiles + t].astype(F32) + p2r[1, t].astype(F32)
        ).astype(BF)
        y1(1, tiles + t).wait_recv()
        y2(0, t).wait_recv()
        out_ref[pl.ds(top, top), lanes] = (
            own[t, pl.ds(top, top), :] + p1r[1, tiles + t].astype(F32) + p2r[0, t].astype(F32)
        ).astype(BF)
        return 0

    lax.fori_loop(0, tiles, last, 0)
    for c in range(parts):

        def last_given(t, _):
            lanes = pl.ds(pl.multiple_of(t * tw, tw), tw)
            h2(c, t).wait_recv()
            out_ref[pl.ds(lead + c * part, part), lanes] = (
                ownh[c, t] + h2r[c, t].astype(F32)
            ).astype(BF)
            return 0

        lax.fori_loop(0, tiles, last_given, 0)

    for i in range(fetches):
        w_fetch(i).wait_send()
    for c in range(parts):
        normed_copy(c).wait_send()

        def drain3(t, _):
            h2(c, t).wait_send()
            return 0

        lax.fori_loop(0, tiles, drain3, 0)

    for i in range(1, LINE):
        send1((d + i) % LINE).wait_send()

    @pl.when(core == 0)
    def _():
        core_copy.wait_send()

    for src in range(PLANES):

        @pl.when(z == src)
        def _():
            for slot, t in enumerate(TAKERS.get(src, ())):
                zcopy(slot, src, t).wait_send()
            for slot, t in enumerate(ROOTS.get(src, ())):
                zcopy(3 + slot, PLANES, t).wait_send()

    for c in range(1, CHIPS):

        @pl.when(x != c)
        def _():
            low_copy(c, c).wait_send()

        @pl.when(x == c)
        def _():
            low_copy(c, 0).wait_send()
            first = 0 if c % 2 else 1
            count = 2 if c == 3 else 1
            rows = pl.ds(128 + first * 128, count * 128)
            for i in range(1, CHIPS):
                spread(
                    states.at[0, rows, :], rows, mate, low_s, CHIPS + i - 1, low_r, 0
                ).wait_send()

    for cp in sends:
        cp.wait_send()
    for side in range(2):

        def drain(i, _):
            y1(side, i).wait_send()
            return 0

        lax.fori_loop(0, 2 * tiles, drain, 0)

        def drain2(i, _):
            y2(side, i).wait_send()
            return 0

        lax.fori_loop(0, tiles, drain2, 0)


def local(queries, keys, values, level_weights, out_weight):
    tok, width = queries.shape
    heads, levels, _ = level_weights.shape
    tiles = 4
    top = 96
    parts = 2
    part = (tok - 2 * top) // parts
    tw = width // tiles
    dma = pltpu.SemaphoreType.DMA
    scratch = [
        pltpu.VMEM((tok, width), BF),
        pltpu.VMEM((tok, width), BF),
        pltpu.VMEM((tok, width), BF),
        pltpu.VMEM((levels, heads, tok), F32),
        pltpu.VMEM((tok, 128), F32),
        pltpu.VMEM(out_weight.shape, BF),
        pltpu.VMEM((heads, 3, 128, 128), BF),
        pltpu.VMEM((heads, 128, 128), BF),
        pltpu.VMEM((LINE, 128, 128), BF),
        pltpu.VMEM((CHIPS, 256, 128), BF),
        pltpu.VMEM((PLANES + 1, 128, 128), BF),
        pltpu.VMEM((heads, FAR * 128, 128), BF),
        pltpu.VMEM((heads, tok, FAR * 128), BF),
        pltpu.VMEM((tok, width), F32),
        pltpu.VMEM((tok, width), BF),
        pltpu.VMEM((2, 2 * tiles, top, tw), BF),
        pltpu.VMEM((2, 2 * tiles, top, tw), BF),
        pltpu.VMEM((2, tiles, top, tw), BF),
        pltpu.VMEM((2, tiles, top, tw), BF),
        pltpu.VMEM((2, tiles, top, tw), F32),
        pltpu.VMEM((tiles, 2 * top, tw), F32),
        pltpu.VMEM((2, width, width), BF),
        pltpu.VMEM((parts, part, width), BF),
        pltpu.VMEM((parts, tiles, part, tw), BF),
        pltpu.VMEM((parts, tiles, part, tw), BF),
        pltpu.VMEM((parts, tiles, part, tw), F32),
        dma((5,)),
        dma((LINE,)),
        dma((LINE,)),
        dma,
        dma,
        dma((5,)),
        dma((PLANES + 1,)),
        dma((2 * CHIPS,)),
        dma((LINE,)),
        dma((2 * CHIPS,)),
        dma((LINE,)),
        dma((2 * CHIPS,)),
        dma((LINE,)),
        dma((2, 2 * tiles)),
        dma((2, 2 * tiles)),
        dma((2, tiles)),
        dma((2, tiles)),
        dma((4,)),
        dma((8, 2)),
        dma((LINE + 2, 2)),
        dma((parts,)),
        dma((parts,)),
        dma((parts, tiles)),
        dma((parts, tiles)),
    ]
    return pl.pallas_call(
        kernel,
        out_shape=pltpu.VMEM((tok, width), BF),
        in_specs=[pl.BlockSpec(memory_space=pl.ANY)] * 5,
        out_specs=pl.BlockSpec(memory_space=pltpu.VMEM),
        scratch_shapes=scratch,
        compiler_params=pltpu.CompilerParams(
            collective_id=0, has_side_effects=True, vmem_limit_bytes=60 * 1024 * 1024
        ),
    )(queries, keys, values, level_weights.transpose(1, 0, 2), out_weight)


def solution(mesh):
    in_specs = (
        P("seq", "head"),
        P("seq", "head"),
        P("seq", "head"),
        P("head", None, "seq"),
        P("head", None),
    )
    out_specs = P("seq", "head")
    return jax.shard_map(local, mesh=mesh, in_specs=in_specs, out_specs=out_specs, check_vma=False)
```
